32 devices in a mesh: leaf: 8 (over z, y), rhs: 4 (over x, core).
Axes of the slice: x: 2, y: 2, z: 4, core: 2. Of those that a mesh axis runs over, the one named last changes fastest.
Arguments:
- leaf_parents: int32 [32], replicated, may hold values from 0 to 15, as said below
- mid_parents: int32 [16], replicated, may hold values from 0 to 7, as said below
- leaf_codes: int32 [32, 1], replicated, may hold values from 0 to 7, as said below
- mid_codes: int32 [16, 1], replicated, may hold values from 0 to 3, as said below
- leaf_valid: int32 [32], P('leaf'), may hold values from 1 to 128
- mid_valid: int32 [16], P('leaf'), may hold values from 1 to 128
- leaf_inverse: bfloat16 [32, 512, 512], P('leaf')
- mid_inverse: bfloat16 [16, 512, 512], P('leaf')
- top_inverse: bfloat16 [8, 512, 512], P('leaf')
- leaf_panels: bfloat16 [32, 128, 512], P('leaf'), may hold values from -0.1875 to 0.1875
- mid_panels: bfloat16 [16, 128, 512], P('leaf'), may hold values from -0.1875 to 0.1875
- leaf_cotangent: bfloat16 [32, 128, 512], P('leaf', 'rhs'), may hold values from -6 to 6
- mid_cotangent: bfloat16 [16, 128, 512], P('leaf', 'rhs'), may hold values from -6 to 6
- top_cotangent: bfloat16 [8, 128, 512], P('leaf', 'rhs'), may hold values from -6 to 6
- mid_primal: bfloat16 [16, 128, 512], P('leaf', 'rhs'), may hold values from -0.59765625 to 0.59765625
- top_primal: bfloat16 [8, 128, 512], P('leaf', 'rhs'), may hold values from -0.59765625 to 0.59765625
Outputs:
- leaf_adjoint: bfloat16 [32, 128, 512], P('leaf', 'rhs')
- mid_adjoint: bfloat16 [16, 128, 512], P('leaf', 'rhs')
- top_adjoint: bfloat16 [8, 128, 512], P('leaf', 'rhs')
- leaf_grad: bfloat16 [32, 128, 512], P('leaf', 'rhs')
- mid_grad: bfloat16 [16, 128, 512], P('leaf', 'rhs')
The draws below stay inside these ranges and needn't reach their ends.
Inputs may be any that keep to these rules, and one draw needn't show every extreme that they name: `leaf_parents`: the parent of level-0 supernode s is level-1 supernode s // 2 or one beside it. `mid_parents`: the parent of level-1 supernode p is level-2 supernode p // 2 or one beside it; it is p // 2 + 1 whenever p % 4 == 3 and p < 15. `leaf_codes`: the 1 codes of one panel are distinct. `mid_codes`: the 1 codes of one panel are distinct.
All inputs are finite; a program needn't handle non-finite values.
Results may differ from the reference program's by a relative error of at most 0.0053.
Values may be sent and summed in bfloat16 or wider, within the bound.
No kernel may reach another device: no remote copies, remote signals or barrier semaphores. Data moves between devices by JAX's collectives and lax.ppermute only.
A program may use at most 64 MiB of HBM per device.

```python
import math
import jax
import jax.numpy as jnp
from jax import lax

W = 512
BLK = 128
MB = 1
RHS = 128
MR = 128
NB = 4
NL0 = 32
NL1 = 16
NL2 = 8


def node_parents(key, count, upper, bridge):
    nodes = jnp.arange(count, dtype=jnp.int32)
    offsets = jax.random.randint(key, (count,), -1, 2, dtype=jnp.int32)
    if bridge:
        offsets = jnp.where(nodes % 4 == 3, 1, offsets)
    offsets = jnp.where((nodes == 0) | (nodes == count - 1), 0, offsets)
    return jnp.clip(nodes // 2 + offsets, 0, upper - 1).astype(jnp.int32)


def block_codes(key, count, span):
    score_key, spot_key = jax.random.split(key)
    scores = jax.random.randint(score_key, (count, span), 0, 1 << 20, dtype=jnp.int32) * span + jnp.arange(span, dtype=jnp.int32)[None, :]
    spot = jax.random.randint(spot_key, (), 0, count, dtype=jnp.int32)
    rows = jnp.arange(count, dtype=jnp.int32)[:, None]
    cols = jnp.arange(span, dtype=jnp.int32)[None, :]
    scores = jnp.where((rows == spot) & (cols == span - 1), -1, scores)
    scores = jnp.where((rows == (spot + 1) % count) & (cols == 0), -1, scores)
    return jnp.argsort(scores, axis=1, stable=True)[:, :MB].astype(jnp.int32)


def row_counts(key, count):
    count_key, spot_key, gap_key = jax.random.split(key, 3)
    counts = jax.random.randint(count_key, (count,), 1, MR + 1, dtype=jnp.int32)
    spot = jax.random.randint(spot_key, (), 0, count, dtype=jnp.int32)
    gap = jax.random.randint(gap_key, (), 1, count, dtype=jnp.int32)
    nodes = jnp.arange(count, dtype=jnp.int32)
    counts = jnp.where(nodes == spot, MR, counts)
    counts = jnp.where(nodes == (spot + gap) % count, 1, counts)
    return counts.astype(jnp.int32)


def factor_inverse(key, count):
    diag_key, off_key = jax.random.split(key)
    rows = jnp.arange(W, dtype=jnp.int32)
    spread = jax.random.normal(off_key, (count, W, W), jnp.float32)
    diagonal = jax.random.uniform(diag_key, (count, W, 1), jnp.float32, 0.7, 1.4)
    lower_part = rows[:, None] > rows[None, :]
    on_diag = rows[:, None] == rows[None, :]
    result = jnp.where(lower_part, spread * (0.4 / math.sqrt(W)), 0.0)
    return jnp.where(on_diag, diagonal, result).astype(jnp.float32)


def draw_leaf_parents(key, part):
    return node_parents(jax.random.fold_in(key, 11), NL0, NL1, False)


def draw_mid_parents(key, part):
    return node_parents(jax.random.fold_in(key, 12), NL1, NL2, True)


def draw_leaf_codes(key, part):
    return block_codes(jax.random.fold_in(key, 21), NL0, 2 * NB)


def draw_mid_codes(key, part):
    return block_codes(jax.random.fold_in(key, 22), NL1, NB)


def draw_leaf_valid(key, part):
    return row_counts(jax.random.fold_in(key, 31), NL0)


def draw_mid_valid(key, part):
    return row_counts(jax.random.fold_in(key, 32), NL1)


def draw_leaf_inverse(key, part):
    return factor_inverse(jax.random.fold_in(key, 41), NL0).astype(jnp.bfloat16)


def draw_mid_inverse(key, part):
    return factor_inverse(jax.random.fold_in(key, 42), NL1).astype(jnp.bfloat16)


def draw_top_inverse(key, part):
    return factor_inverse(jax.random.fold_in(key, 43), NL2).astype(jnp.bfloat16)


def steps_of(key, extent, shards, least, largest):
    loudness, own = 1.0, jax.random.fold_in(key, 6)
    for position, blocks in shards:
        heights = jnp.exp(jax.random.uniform(jax.random.fold_in(own, position), (blocks,), jnp.float32, least / len(shards), largest / len(shards)))
        loudness = loudness * jnp.repeat(heights, extent[position] // blocks).reshape([-1 if axis == position else 1 for axis in range(len(extent))])
    return loudness


def scatter_about(own_key, dims, scale, limit, cuts=(), kind=jnp.bfloat16):
    factor_of = steps_of(own_key, dims, cuts, -0.22, 0.18) if cuts else 1.0
    drawn = jax.random.normal(own_key, dims, jnp.float32) * scale * factor_of
    return jnp.minimum(jnp.maximum(drawn, -limit), limit).astype(kind)


def setup_inputs(seed: int = 0) -> dict:
    key_list = jax.random.split(jax.random.key(seed), 17)
    return {
        "leaf_parents": draw_leaf_parents(jax.random.fold_in(key_list[16], 71), 0),
        "mid_parents": draw_mid_parents(jax.random.fold_in(key_list[16], 71), 0),
        "leaf_codes": draw_leaf_codes(jax.random.fold_in(key_list[16], 71), 0),
        "mid_codes": draw_mid_codes(jax.random.fold_in(key_list[16], 71), 0),
        "leaf_valid": draw_leaf_valid(jax.random.fold_in(key_list[16], 71), 0),
        "mid_valid": draw_mid_valid(jax.random.fold_in(key_list[16], 71), 0),
        "leaf_inverse": draw_leaf_inverse(jax.random.fold_in(key_list[16], 71), 0),
        "mid_inverse": draw_mid_inverse(jax.random.fold_in(key_list[16], 71), 0),
        "top_inverse": draw_top_inverse(jax.random.fold_in(key_list[16], 71), 0),
        "leaf_panels": scatter_about(key_list[9], (NL0, MR, W), (2 * W) ** -0.5, 0.1875, ((0, 8),)),
        "mid_panels": scatter_about(key_list[10], (NL1, MR, W), (2 * W) ** -0.5, 0.1875, ((0, 8),)),
        "leaf_cotangent": scatter_about(key_list[11], (NL0, RHS, W), 1.0, 6.0, ((0, 8), (1, 4))),
        "mid_cotangent": scatter_about(key_list[12], (NL1, RHS, W), 1.0, 6.0, ((0, 8), (1, 4))),
        "top_cotangent": scatter_about(key_list[13], (NL2, RHS, W), 1.0, 6.0, ((0, 8), (1, 4))),
        "mid_primal": scatter_about(key_list[14], (NL1, RHS, W), 0.1, 0.59765625, ((0, 8), (1, 4))),
        "top_primal": scatter_about(key_list[15], (NL2, RHS, W), 0.1, 0.59765625, ((0, 8), (1, 4))),
    }


def solve_all(block_rows, inverse):
    def single(pair):
        return jnp.dot(pair[0], pair[1].T, preferred_element_type=jnp.float32)
    return lax.map(single, (block_rows, inverse))


def mask_columns(block_rows, row_limit):
    columns = jnp.arange(block_rows.shape[2], dtype=jnp.int32)
    return jnp.where(columns[None, None, :] < row_limit[:, None, None], block_rows, jnp.zeros_like(block_rows))


def update_all(adjoint_rows, panel_rows, row_limit):
    def single(pair):
        return jnp.dot(pair[0], pair[1].T, preferred_element_type=jnp.float32)
    return mask_columns(lax.map(single, (adjoint_rows, panel_rows)), row_limit)


def tile(pair):
    return -jnp.dot(pair[0].T, pair[1], preferred_element_type=jnp.float32)


def reference(leaf_parents, mid_parents, leaf_codes, mid_codes, leaf_valid, mid_valid, leaf_inverse, mid_inverse, top_inverse, leaf_panels, mid_panels, leaf_cotangent, mid_cotangent, top_cotangent, mid_primal, top_primal):
    leaf_total = leaf_parents.shape[0]
    mid_total = mid_parents.shape[0]
    top_total = top_cotangent.shape[0]
    leaf_adjoint = solve_all(leaf_cotangent, leaf_inverse).astype(jnp.bfloat16)
    leaf_update = update_all(leaf_adjoint, leaf_panels, leaf_valid)
    leaf_grand = mid_parents[leaf_parents].astype(jnp.int32)
    to_grand = leaf_codes >= NB
    pieces = leaf_update.reshape(leaf_total, RHS, MB, BLK).transpose(0, 2, 1, 3)
    near_pieces = jnp.where(to_grand[:, :, None, None], 0.0, pieces)
    far_pieces = jnp.where(to_grand[:, :, None, None], pieces, 0.0)
    near_block = jnp.clip(leaf_codes, 0, NB - 1).astype(jnp.int32)
    far_block = jnp.clip(leaf_codes - NB, 0, NB - 1).astype(jnp.int32)
    parent_index = jnp.broadcast_to(leaf_parents[:, None], (leaf_total, MB)).astype(jnp.int32)
    grand_index = jnp.broadcast_to(leaf_grand[:, None], (leaf_total, MB)).astype(jnp.int32)
    mid_from_leaf = jnp.zeros((mid_total, RHS, NB, BLK), jnp.float32).at[parent_index, :, near_block, :].add(near_pieces)
    top_from_leaf = jnp.zeros((top_total, RHS, NB, BLK), jnp.float32).at[grand_index, :, far_block, :].add(far_pieces)
    middle_accum = mid_cotangent.astype(jnp.float32) - mid_from_leaf.reshape(mid_total, RHS, W)
    mid_adjoint = solve_all(middle_accum.astype(jnp.bfloat16), mid_inverse).astype(jnp.bfloat16)
    middle_update = update_all(mid_adjoint, mid_panels, mid_valid)
    mid_pieces = middle_update.reshape(mid_total, RHS, MB, BLK).transpose(0, 2, 1, 3)
    mid_index = jnp.broadcast_to(mid_parents[:, None], (mid_total, MB)).astype(jnp.int32)
    top_from_mid = jnp.zeros((top_total, RHS, NB, BLK), jnp.float32).at[mid_index, :, mid_codes, :].add(mid_pieces)
    top_accum = top_cotangent.astype(jnp.float32) - top_from_leaf.reshape(top_total, RHS, W) - top_from_mid.reshape(top_total, RHS, W)
    top_adjoint = solve_all(top_accum.astype(jnp.bfloat16), top_inverse).astype(jnp.bfloat16)
    parent_blocks = mid_primal.reshape(mid_total, RHS, NB, BLK)
    grand_blocks = top_primal.reshape(top_total, RHS, NB, BLK)
    near_pick = parent_blocks[parent_index, :, near_block, :]
    far_pick = grand_blocks[grand_index, :, far_block, :]
    leaf_rows = jnp.where(to_grand[:, :, None, None], far_pick, near_pick).transpose(0, 2, 1, 3).reshape(leaf_total, RHS, MR)
    leaf_rows = mask_columns(leaf_rows, leaf_valid)
    mid_rows = grand_blocks[mid_index, :, mid_codes, :].transpose(0, 2, 1, 3).reshape(mid_total, RHS, MR)
    mid_rows = mask_columns(mid_rows, mid_valid)
    leaf_grad = lax.map(tile, (leaf_rows, leaf_adjoint)).astype(jnp.bfloat16)
    mid_grad = lax.map(tile, (mid_rows, mid_adjoint)).astype(jnp.bfloat16)
    return (leaf_adjoint, mid_adjoint, top_adjoint, leaf_grad, mid_grad)
```

```python
import jax
import jax.numpy as jnp
from jax import lax
from jax.experimental import pallas as pl
from jax.experimental.pallas import tpu as pltpu
from jax.sharding import PartitionSpec as P

BLK = 128
NB = 4
FAN = 2
BF16 = jnp.bfloat16
F32 = jnp.float32
SMEM = pl.BlockSpec(memory_space=pltpu.SMEM)
VMEM = pl.BlockSpec(memory_space=pltpu.VMEM)


def dot_t(a, b):
    return lax.dot_general(a, b, (((1,), (1,)), ((), ())), preferred_element_type=F32)


def div(a, b):
    return lax.div(a, jnp.int32(b))


def swaps(size, first, stride):
    pairs = []
    for i in range(size):
        block = i // stride
        other = i + stride if (block - first) % 2 == 0 else i - stride
        if 0 <= other < size:
            pairs.append((i, other))
    return pairs


def partner(d, first, stride):
    block = div(d, stride)
    return jnp.where((block - first) % 2 == 0, d + stride, d - stride)


def clip(i, size):
    return jnp.minimum(jnp.maximum(i, 0), size - 1)


class Tables:
    def __init__(self, lp, mp, lc, mc, nl, nm, nt):
        self.lp, self.mp, self.lc, self.mc = lp, mp, lc, mc
        self.nl, self.nm, self.nt = nl, nm, nt

    def leaf(self, s):
        s = clip(s, self.lp.shape[0])
        p = self.lp[s]
        code = self.lc[s]
        q = self.mp[p]
        return p, q, code

    def leaf_source(self, s):
        p, q, code = self.leaf(s)
        near = code < NB
        device = jnp.where(near, div(p, self.nm), div(q, self.nt))
        row = jnp.where(near, p - div(p, self.nm) * self.nm, q - div(q, self.nt) * self.nt)
        return near, device, row, jnp.where(near, code, code - NB)

    def mid_source(self, m):
        m = clip(m, self.mp.shape[0])
        q = self.mp[m]
        return div(q, self.nt), q - div(q, self.nt) * self.nt, self.mc[m]


def block_of(ref, row, blk):
    return ref[row, :, pl.ds(pl.multiple_of(blk * BLK, BLK), BLK)]


def leaf_pick(tabs, s, mprim, tprim):
    near, _, row, blk = tabs.leaf_source(s)
    a = block_of(mprim, jnp.where(near, row, 0), blk)
    b = block_of(tprim, jnp.where(near, 0, row), blk)
    return jnp.where(near, a, b)


def mid_pick(tabs, m, tprim):
    _, row, blk = tabs.mid_source(m)
    return block_of(tprim, row, blk)


def leaf_kernel(lp, mp, lc, mc, lv, cot, inv, pan, mprim, tprim,
                adj, upd, send_z, send_y, far_a, far_b):
    nl, nm, nt = cot.shape[0], mprim.shape[0], tprim.shape[0]
    d = lax.axis_index("leaf")
    tabs = Tables(lp, mp, lc, mc, nl, nm, nt)
    col = lax.broadcasted_iota(jnp.int32, upd.shape[1:], 1)
    for s in range(nl):
        a = dot_t(cot[s], inv[s]).astype(BF16)
        adj[s] = a
        u = dot_t(a, pan[s])
        upd[s] = jnp.where(col < lv[s], u, 0.0)
    for out, first in ((send_z, 1), (send_y, 0)):
        t = partner(d, first, 1)
        start = jnp.where(t > d, nl - FAN, 0)
        for i in range(FAN):
            out[i] = upd[start + i].astype(BF16)
        for i in range(nl):
            out[FAN + i] = leaf_pick(tabs, t * nl + i, mprim, tprim)
        for i in range(nm):
            out[FAN + nl + i] = mid_pick(tabs, t * nm + i, tprim)
    for out, first in ((far_a, 0), (far_b, 1)):
        t = partner(d, first, 2)
        start = jnp.where(t > d, 0, nl - FAN)
        for i in range(FAN):
            _, _, row, blk = tabs.leaf_source(t * nl + start + i)
            out[i] = block_of(tprim, jnp.minimum(row, nt - 1), blk)


def mid_kernel(lp, mp, lc, mc, lv, mv, rec_z, rec_y, far_a, far_b, upd, cot, inv, pan,
               mprim, tprim, adj, rows, send_z, send_y, keep, acc):
    nl, nm, nt = upd.shape[0], mprim.shape[0], tprim.shape[0]
    d = lax.axis_index("leaf")
    tabs = Tables(lp, mp, lc, mc, nl, nm, nt)
    base = nm * NB
    dump = base + 3 * nt * NB
    for m in range(nm):
        for k in range(NB):
            acc[m * NB + k] = cot[m, :, k * BLK:(k + 1) * BLK].astype(F32)
    for k in range(base, dump):
        acc[k] = jnp.zeros(acc.shape[1:], F32)
    total = lp.shape[0]

    def top_slot(q, k):
        return base + (q - (d - 1) * nt) * NB + k

    def take(s, value):
        p, q, code = tabs.leaf(s)
        mine = (s >= 0) & (s < total) & (div(p, nm) == d)
        slot = jnp.where(code < NB, (p - d * nm) * NB + code, top_slot(q, code - NB))
        slot = jnp.where(mine, slot, dump)
        acc[slot] = acc[slot] - value

    for i in range(nl):
        take(d * nl + i, upd[i])
    near = []
    for rec, first in ((rec_z, 1), (rec_y, 0)):
        t = partner(d, first, 1)
        near.append((t, rec))
        start = jnp.where(t > d, t * nl, (t + 1) * nl - FAN)
        for i in range(FAN):
            take(start + i, rec[i].astype(F32))
    col = lax.broadcasted_iota(jnp.int32, acc.shape[1:], 1)
    for m in range(nm):
        rhs = jnp.concatenate([acc[m * NB + k].astype(BF16) for k in range(NB)], axis=1)
        a = dot_t(rhs, inv[m]).astype(BF16)
        adj[m] = a
        u = jnp.where(col < mv[m], dot_t(a, pan[m]), 0.0)
        p = d * nm + m
        slot = top_slot(mp[p], mc[p])
        acc[slot] = acc[slot] - u
    for out, (t, _) in ((send_z, near[0]), (send_y, near[1])):
        for k in range(nt * NB):
            out[k] = acc[base + (t - d + 1) * nt * NB + k].astype(BF16)
    for k in range(nt * NB):
        keep[k] = acc[base + nt * NB + k]
    far = ((partner(d, 0, 2), far_a), (partner(d, 1, 2), far_b))
    for i in range(nl):
        _, dev, _, _ = tabs.leaf_source(d * nl + i)
        value = leaf_pick(tabs, d * nl + i, mprim, tprim)
        for t, rec in near:
            value = jnp.where(dev == t, rec[FAN + i], value)
        for t, rec in far:
            if i < FAN:
                value = jnp.where((dev == t) & (t < d), rec[i], value)
            if i >= nl - FAN:
                value = jnp.where((dev == t) & (t > d), rec[i - nl + FAN], value)
        rows[i] = jnp.where(col < lv[i], value, jnp.zeros_like(value))
    for i in range(nm):
        dev, _, _ = tabs.mid_source(d * nm + i)
        value = mid_pick(tabs, d * nm + i, tprim)
        for t, rec in near:
            value = jnp.where(dev == t, rec[FAN + nl + i], value)
        rows[nl + i] = jnp.where(col < mv[i], value, jnp.zeros_like(value))


def grad_kernel(groups, leaf_own, leaf_other, mid_own, mid_other, rows_own, rows_other,
                *outs):
    keep, sends, cols = outs[0], outs[1:-1], outs[-1]
    nl = leaf_own.shape[0]
    j = lax.axis_index("rhs")
    x = div(j, 2)
    width = keep.shape[1]
    for s in range(rows_own.shape[0]):
        own, other, i = (leaf_own, leaf_other, s) if s < nl else (mid_own, mid_other, s - nl)
        both = jnp.concatenate([rows_own[s], rows_other[s]], axis=0)
        adj = jnp.concatenate([own[i], other[i]], axis=0)
        cols[...] = lax.dot_general(
            both, adj, (((0,), (0,)), ((), ())), preferred_element_type=F32
        )
        keep[s] = cols[pl.ds(pl.multiple_of(j * width, width), width), :]
        for step, out in enumerate(sends, 1):
            to = (x + step) % groups * 2 + j % 2
            out[s] = cols[pl.ds(pl.multiple_of(to * width, width), width), :].astype(BF16)


def top_kernel(keep, rec_z, rec_y, cot, inv, adj):
    nt = cot.shape[0]
    for q in range(nt):
        parts = []
        for k in range(NB):
            total = keep[q * NB + k] + rec_z[q * NB + k].astype(F32) + rec_y[q * NB + k].astype(F32)
            total = total + cot[q, :, k * BLK:(k + 1) * BLK].astype(F32)
            parts.append(total.astype(BF16))
        adj[q] = dot_t(jnp.concatenate(parts, axis=1), inv[q]).astype(BF16)


def call(kernel, name, tables, arrays, outs, scratch=()):
    return pl.pallas_call(
        kernel,
        name=name,
        out_shape=[jax.ShapeDtypeStruct(s, t) for s, t in outs],
        in_specs=[SMEM] * len(tables) + [VMEM] * len(arrays),
        out_specs=[VMEM] * len(outs),
        scratch_shapes=list(scratch),
    )(*tables, *arrays)


def shards(leaf_parents, mid_parents, leaf_codes, mid_codes, leaf_valid, mid_valid,
           leaf_inverse, mid_inverse, top_inverse, leaf_panels, mid_panels,
           leaf_cotangent, mid_cotangent, top_cotangent, mid_primal, top_primal):
    nl, probes, width = leaf_cotangent.shape
    nm = mid_cotangent.shape[0]
    nt = top_cotangent.shape[0]
    rows = leaf_panels.shape[1]
    leaves = lax.axis_size("leaf")
    peers = lax.axis_size("rhs")
    groups = peers // 2
    assert leaf_codes.shape[1] == 1 and mid_codes.shape[1] == 1 and rows == BLK
    tables = (leaf_parents, mid_parents, leaf_codes.reshape(-1), mid_codes.reshape(-1))
    load = FAN + nl + nm

    def along(value, first, stride):
        return lax.ppermute(value, "leaf", swaps(leaves, first, stride))

    def core_swap(value):
        return lax.ppermute(value, "rhs", [(i, i ^ 1) for i in range(peers)])

    piece = (probes, BLK)
    leaf_adj, upd, send_z, send_y, far_a, far_b = call(
        leaf_kernel, "leaf", (*tables, leaf_valid),
        (leaf_cotangent, leaf_inverse, leaf_panels, mid_primal, top_primal),
        [((nl, probes, width), BF16), ((nl, *piece), F32), ((load, *piece), BF16),
         ((load, *piece), BF16), ((FAN, *piece), BF16), ((FAN, *piece), BF16)],
    )
    rec_z = along(send_z, 1, 1)
    rec_y = along(send_y, 0, 1)
    far_a = along(far_a, 0, 2)
    far_b = along(far_b, 1, 2)
    leaf_other = core_swap(leaf_adj)
    mid_adj, row_blocks, send_z, send_y, keep = call(
        mid_kernel, "mid", (*tables, leaf_valid, mid_valid),
        (rec_z, rec_y, far_a, far_b, upd, mid_cotangent, mid_inverse, mid_panels,
         mid_primal, top_primal),
        [((nm, probes, width), BF16), ((nl + nm, *piece), BF16), ((nt * NB, *piece), BF16),
         ((nt * NB, *piece), BF16), ((nt * NB, *piece), F32)],
        [pltpu.VMEM((nm * NB + 3 * nt * NB + 1, *piece), F32)],
    )
    rec_z = along(send_z, 1, 1)
    rec_y = along(send_y, 0, 1)
    mid_other = core_swap(mid_adj)
    rows_other = core_swap(row_blocks)
    part = (nl + nm, rows // peers, width)
    own, *sends = call(
        lambda *refs: grad_kernel(groups, *refs), "grad", (),
        (leaf_adj, leaf_other, mid_adj, mid_other, row_blocks, rows_other),
        [(part, F32)] + [(part, BF16)] * (groups - 1),
        [pltpu.VMEM((rows, width), F32)],
    )
    for step, value in enumerate(sends, 1):
        pairs = [(i, (i // 2 + step) % groups * 2 + i % 2) for i in range(peers)]
        own = own + lax.ppermute(value, "rhs", pairs).astype(F32)
    (top_adj,) = call(
        top_kernel, "top", (), (keep, rec_z, rec_y, top_cotangent, top_inverse),
        [((nt, probes, width), BF16)],
    )
    grad = -own
    return leaf_adj, mid_adj, top_adj, grad[:nl].astype(BF16), grad[nl:].astype(BF16)


def solution(mesh):
    each = P("leaf")
    block = P("leaf", None, None)
    split = P("leaf", "rhs", None)
    return jax.shard_map(
        shards,
        mesh=mesh,
        in_specs=(P(),) * 4 + (each,) * 2 + (block,) * 5 + (split,) * 5,
        out_specs=(split,) * 5,
        check_vma=False,
    )
```

```python
import jax
import jax.numpy as jnp
from jax import lax
from jax.experimental import pallas as pl
from jax.experimental.pallas import tpu as pltpu
from jax.sharding import PartitionSpec as P

BLK = 128
NB = 4
FAN = 2
LIMIT = 16 << 20
BF16 = jnp.bfloat16
F32 = jnp.float32


def dot_t(a, b):
    return lax.dot_general(a, b, (((1,), (1,)), ((), ())), preferred_element_type=F32)


def div(a, b):
    return lax.div(a, jnp.int32(b))


def swaps(size, first, stride):
    pairs = []
    for i in range(size):
        block = i // stride
        other = i + stride if (block - first) % 2 == 0 else i - stride
        if 0 <= other < size:
            pairs.append((i, other))
    return pairs


def partner(d, first, stride):
    block = div(d, stride)
    return jnp.where((block - first) % 2 == 0, d + stride, d - stride)


def clip(i, size):
    return jnp.minimum(jnp.maximum(i, 0), size - 1)


class Tables:
    def __init__(self, lp, mp, lc, mc, nl, nm, nt):
        self.lp, self.mp, self.lc, self.mc = lp, mp, lc, mc
        self.nl, self.nm, self.nt = nl, nm, nt

    def leaf(self, s):
        s = clip(s, self.lp.shape[0])
        p = self.lp[s]
        code = self.lc[s]
        q = self.mp[p]
        return p, q, code

    def leaf_source(self, s):
        p, q, code = self.leaf(s)
        near = code < NB
        device = jnp.where(near, div(p, self.nm), div(q, self.nt))
        row = jnp.where(near, p - div(p, self.nm) * self.nm, q - div(q, self.nt) * self.nt)
        return near, device, row, jnp.where(near, code, code - NB)

    def mid_source(self, m):
        m = clip(m, self.mp.shape[0])
        q = self.mp[m]
        return div(q, self.nt), q - div(q, self.nt) * self.nt, self.mc[m]


def block_of(ref, row, blk):
    return ref[row, :, pl.ds(pl.multiple_of(blk * BLK, BLK), BLK)]


def leaf_pick(tabs, s, mprim, tprim):
    near, _, row, blk = tabs.leaf_source(s)
    a = block_of(mprim, jnp.where(near, row, 0), blk)
    b = block_of(tprim, jnp.where(near, 0, row), blk)
    return jnp.where(near, a, b)


def mid_pick(tabs, m, tprim):
    _, row, blk = tabs.mid_source(m)
    return block_of(tprim, row, blk)


def leaf_kernel(lp_h, mp_h, lc_h, mc_h, lv_h, mv_h, cot_h, inv_h, pan_h, mprim_h, tprim_h,
                later_a, later_b, later_c, later_d, later_e, lp, mp, lc, mc, lv, mv,
                adj, upd, send_z, send_y, far_a, far_b, mprim, tprim,
                out_a, out_b, out_c, out_d, out_e, cot, inv, pan, sems, table_sems):
    nl, nm, nt = cot.shape[0], mprim.shape[0], tprim.shape[0]
    pairs = [(cot_h, cot)]
    for s in range(nl):
        pairs += [(inv_h.at[s], inv.at[s]), (pan_h.at[s], pan.at[s])]
    pairs += [(mprim_h, mprim), (tprim_h, tprim), (later_a, out_a), (later_b, out_b),
              (later_c, out_c), (later_d, out_d), (later_e, out_e)]
    copies = [pltpu.make_async_copy(*pair, sems.at[i]) for i, pair in enumerate(pairs)]
    for copy in copies[:2]:
        copy.start()
    pairs = [(lp_h, lp), (mp_h, mp), (lc_h, lc), (mc_h, mc), (lv_h, lv), (mv_h, mv)]
    reads = [pltpu.make_async_copy(*pair, table_sems.at[i]) for i, pair in enumerate(pairs)]
    for copy in reads + copies[2:]:
        copy.start()
    d = lax.axis_index("leaf")
    tabs = Tables(lp, mp, lc, mc, nl, nm, nt)
    col = lax.broadcasted_iota(jnp.int32, upd.shape[1:], 1)
    for copy in reads:
        copy.wait()
    copies[0].wait()
    for s in range(nl):
        copies[1 + 2 * s].wait()
        a = dot_t(cot[s], inv[s]).astype(BF16)
        adj[s] = a
        copies[2 + 2 * s].wait()
        u = dot_t(a, pan[s])
        upd[s] = jnp.where(col < lv[s], u, 0.0)
    copies[1 + 2 * nl].wait()
    copies[2 + 2 * nl].wait()
    for out, first in ((send_z, 1), (send_y, 0)):
        t = partner(d, first, 1)
        start = jnp.where(t > d, nl - FAN, 0)
        for i in range(FAN):
            out[i] = upd[start + i].astype(BF16)
        for i in range(nl):
            out[FAN + i] = leaf_pick(tabs, t * nl + i, mprim, tprim)
        for i in range(nm):
            out[FAN + nl + i] = mid_pick(tabs, t * nm + i, tprim)
    for out, first in ((far_a, 0), (far_b, 1)):
        t = partner(d, first, 2)
        start = jnp.where(t > d, 0, nl - FAN)
        for i in range(FAN):
            _, _, row, blk = tabs.leaf_source(t * nl + start + i)
            out[i] = block_of(tprim, jnp.minimum(row, nt - 1), blk)
    for copy in copies[3 + 2 * nl:]:
        copy.wait()


def mid_kernel(lp, mp, lc, mc, lv, mv, rec_z, rec_y, far_a, far_b, upd, cot, inv, pan,
               mprim, tprim, adj, rows, send_z, send_y, keep, acc):
    nl, nm, nt = upd.shape[0], mprim.shape[0], tprim.shape[0]
    d = lax.axis_index("leaf")
    tabs = Tables(lp, mp, lc, mc, nl, nm, nt)
    base = nm * NB
    dump = base + 3 * nt * NB
    for m in range(nm):
        for k in range(NB):
            acc[m * NB + k] = cot[m, :, k * BLK:(k + 1) * BLK].astype(F32)
    for k in range(base, dump):
        acc[k] = jnp.zeros(acc.shape[1:], F32)
    total = lp.shape[0]

    def top_slot(q, k):
        return clip(base + (q - (d - 1) * nt) * NB + k, dump)

    def take(s, value):
        p, q, code = tabs.leaf(s)
        mine = (s >= 0) & (s < total) & (div(p, nm) == d)
        slot = jnp.where(code < NB, (p - d * nm) * NB + code, top_slot(q, code - NB))
        slot = jnp.where(mine, clip(slot, dump), dump)
        acc[slot] = acc[slot] - value

    for i in range(nl):
        take(d * nl + i, upd[i])
    near = []
    for rec, first in ((rec_z, 1), (rec_y, 0)):
        t = partner(d, first, 1)
        near.append((t, rec))
        start = jnp.where(t > d, t * nl, (t + 1) * nl - FAN)
        for i in range(FAN):
            take(start + i, rec[i].astype(F32))
    col = lax.broadcasted_iota(jnp.int32, acc.shape[1:], 1)
    for m in range(nm):
        rhs = jnp.concatenate([acc[m * NB + k].astype(BF16) for k in range(NB)], axis=1)
        a = dot_t(rhs, inv[m]).astype(BF16)
        adj[m] = a
        u = jnp.where(col < mv[m], dot_t(a, pan[m]), 0.0)
        p = d * nm + m
        slot = top_slot(mp[p], mc[p])
        acc[slot] = acc[slot] - u
    for out, (t, _) in ((send_z, near[0]), (send_y, near[1])):
        for k in range(nt * NB):
            out[k] = acc[base + (t - d + 1) * nt * NB + k].astype(BF16)
    for k in range(nt * NB):
        keep[k] = acc[base + nt * NB + k]
    far = ((partner(d, 0, 2), far_a), (partner(d, 1, 2), far_b))
    for i in range(nl):
        _, dev, _, _ = tabs.leaf_source(d * nl + i)
        value = leaf_pick(tabs, d * nl + i, mprim, tprim)
        for t, rec in near:
            value = jnp.where(dev == t, rec[FAN + i], value)
        for t, rec in far:
            if i < FAN:
                value = jnp.where((dev == t) & (t < d), rec[i], value)
            if i >= nl - FAN:
                value = jnp.where((dev == t) & (t > d), rec[i - nl + FAN], value)
        rows[i] = jnp.where(col < lv[i], value, jnp.zeros_like(value))
    for i in range(nm):
        dev, _, _ = tabs.mid_source(d * nm + i)
        value = mid_pick(tabs, d * nm + i, tprim)
        for t, rec in near:
            value = jnp.where(dev == t, rec[FAN + nl + i], value)
        rows[nl + i] = jnp.where(col < mv[i], value, jnp.zeros_like(value))


def grad_kernel(groups, leaf_own, leaf_other, mid_own, mid_other, rows_own, rows_other,
                leaf_out, mid_out, keep_leaf, keep_mid, *rest):
    sends, cols, sems = rest[:-2], rest[-2], rest[-1]
    copies = [pltpu.make_async_copy(leaf_own, leaf_out, sems.at[0]),
              pltpu.make_async_copy(mid_own, mid_out, sems.at[1])]
    for copy in copies:
        copy.start()
    nl = leaf_own.shape[0]
    j = lax.axis_index("rhs")
    x = div(j, 2)
    width = keep_leaf.shape[1]
    for s in range(rows_own.shape[0]):
        own, other, keep, i = leaf_own, leaf_other, keep_leaf, s
        if s >= nl:
            own, other, keep, i = mid_own, mid_other, keep_mid, s - nl
        both = jnp.concatenate([rows_own[s], rows_other[s]], axis=0)
        adj = jnp.concatenate([own[i], other[i]], axis=0)
        cols[s] = lax.dot_general(
            both, adj, (((0,), (0,)), ((), ())), preferred_element_type=F32
        )
        keep[i] = cols[s, pl.ds(pl.multiple_of(j * width, width), width), :]
        for step, out in enumerate(sends, 1):
            to = (x + step) % groups * 2 + j % 2
            out[s] = cols[s, pl.ds(pl.multiple_of(to * width, width), width), :].astype(BF16)
    for copy in copies:
        copy.wait()


def last_kernel(keep, rec_z, rec_y, cot, inv, leaf_sum, mid_sum, *rest):
    gets, (adj, leaf_out, mid_out) = rest[:-3], rest[-3:]
    nl = leaf_sum.shape[0]
    for total, out, first in ((leaf_sum, leaf_out, 0), (mid_sum, mid_out, nl)):
        for i in range(total.shape[0]):
            value = total[i]
            for get in gets:
                value = value + get[first + i].astype(F32)
            out[i] = (-value).astype(BF16)
    for q in range(cot.shape[0]):
        parts = []
        for k in range(NB):
            total = keep[q * NB + k] + rec_z[q * NB + k].astype(F32) + rec_y[q * NB + k].astype(F32)
            total = total + cot[q, :, k * BLK:(k + 1) * BLK].astype(F32)
            parts.append(total.astype(BF16))
        adj[q] = dot_t(jnp.concatenate(parts, axis=1), inv[q]).astype(BF16)


SPEC = {m: pl.BlockSpec(memory_space=m) for m in (pltpu.SMEM, pltpu.VMEM, pltpu.HBM)}
DMA = pltpu.SemaphoreType.DMA


def call(kernel, name, tables, far, near, outs, scratch=()):
    operands, places = [], []
    for values, place in ((tables, pltpu.SMEM), (far, pltpu.HBM), (near, pltpu.VMEM)):
        operands += [pltpu.with_memory_space_constraint(v, place) for v in values]
        places += [SPEC[place]] * len(values)
    shapes = []
    for shape, dtype, place in outs:
        shapes.append(place(shape, dtype) if place else jax.ShapeDtypeStruct(shape, dtype))
    return pl.pallas_call(
        kernel,
        name=name,
        out_shape=shapes,
        in_specs=places,
        out_specs=[SPEC[place or pltpu.VMEM] for _, _, place in outs],
        scratch_shapes=list(scratch),
        compiler_params=pltpu.CompilerParams(vmem_limit_bytes=LIMIT),
    )(*operands)


def shards(leaf_parents, mid_parents, leaf_codes, mid_codes, leaf_valid, mid_valid,
           leaf_inverse, mid_inverse, top_inverse, leaf_panels, mid_panels,
           leaf_cotangent, mid_cotangent, top_cotangent, mid_primal, top_primal):
    nl, probes, width = leaf_cotangent.shape
    nm = mid_cotangent.shape[0]
    nt = top_cotangent.shape[0]
    rows = leaf_panels.shape[1]
    leaves = lax.axis_size("leaf")
    peers = lax.axis_size("rhs")
    groups = peers // 2
    assert leaf_codes.shape[1] == 1 and mid_codes.shape[1] == 1 and rows == BLK
    tables = (leaf_parents, mid_parents, leaf_codes.reshape(-1), mid_codes.reshape(-1),
              leaf_valid, mid_valid)
    load = FAN + nl + nm

    def along(value, first, stride):
        return lax.ppermute(value, "leaf", swaps(leaves, first, stride))

    def core_swap(value):
        return lax.ppermute(value, "rhs", [(i, i ^ 1) for i in range(peers)])

    def near(shape, dtype):
        return (shape, dtype, pltpu.VMEM)

    def same(value):
        return near(value.shape, value.dtype)

    piece = (probes, BLK)
    moved = (mid_primal, top_primal, mid_cotangent, mid_inverse, mid_panels, top_cotangent,
             top_inverse)
    (*tables, leaf_adj, upd, send_z, send_y, far_a, far_b, mprim, tprim, mid_cot, mid_inv, mid_pan,
     top_cot, top_inv) = call(
        leaf_kernel, "leaf", (),
        (*tables, leaf_cotangent, leaf_inverse, leaf_panels, *moved), (),
        [*((t.shape, t.dtype, pltpu.SMEM) for t in tables),
         near((nl, probes, width), BF16), near((nl, *piece), F32), near((load, *piece), BF16),
         near((load, *piece), BF16), near((FAN, *piece), BF16), near((FAN, *piece), BF16),
         *map(same, moved)],
        [pltpu.VMEM(v.shape, v.dtype) for v in (leaf_cotangent, leaf_inverse, leaf_panels)]
        + [DMA((1 + 2 * nl + len(moved),)), DMA((len(tables),))],
    )
    rec_z = along(send_z, 1, 1)
    rec_y = along(send_y, 0, 1)
    far_a = along(far_a, 0, 2)
    far_b = along(far_b, 1, 2)
    leaf_other = core_swap(leaf_adj)
    mid_adj, row_blocks, send_z, send_y, keep = call(
        mid_kernel, "mid", tables, (),
        (rec_z, rec_y, far_a, far_b, upd, mid_cot, mid_inv, mid_pan, mprim, tprim),
        [near((nm, probes, width), BF16), near((nl + nm, *piece), BF16),
         near((nt * NB, *piece), BF16), near((nt * NB, *piece), BF16),
         near((nt * NB, *piece), F32)],
        [pltpu.VMEM((nm * NB + 3 * nt * NB + 1, *piece), F32)],
    )
    rec_z = along(send_z, 1, 1)
    rec_y = along(send_y, 0, 1)
    mid_other = core_swap(mid_adj)
    rows_other = core_swap(row_blocks)
    part = (rows // peers, width)
    leaf_out, mid_out, leaf_sum, mid_sum, *sends = call(
        lambda *refs: grad_kernel(groups, *refs), "grad", (), (),
        (leaf_adj, leaf_other, mid_adj, mid_other, row_blocks, rows_other),
        [((nl, probes, width), BF16, pltpu.HBM), ((nm, probes, width), BF16, pltpu.HBM),
         near((nl, *part), F32), near((nm, *part), F32)]
        + [near((nl + nm, *part), BF16)] * (groups - 1),
        [pltpu.VMEM((nl + nm, rows, width), F32), DMA((2,))],
    )
    gets = []
    for step, value in enumerate(sends, 1):
        pairs = [(i, (i // 2 + step) % groups * 2 + i % 2) for i in range(peers)]
        gets.append(lax.ppermute(value, "rhs", pairs))
    top_adj, leaf_grad, mid_grad = call(
        last_kernel, "last", (), (),
        (keep, rec_z, rec_y, top_cot, top_inv, leaf_sum, mid_sum, *gets),
        [((nt, probes, width), BF16, None), ((nl, *part), BF16, None), ((nm, *part), BF16, None)],
    )
    return leaf_out, mid_out, top_adj, leaf_grad, mid_grad


def solution(mesh):
    each = P("leaf")
    block = P("leaf", None, None)
    split = P("leaf", "rhs", None)
    return jax.shard_map(
        shards,
        mesh=mesh,
        in_specs=(P(),) * 4 + (each,) * 2 + (block,) * 5 + (split,) * 5,
        out_specs=(split,) * 5,
        check_vma=False,
    )
```

```python
import jax
import jax.numpy as jnp
from jax import lax
from jax.experimental import pallas as pl
from jax.experimental.pallas import tpu as pltpu
from jax.sharding import PartitionSpec as P


BLK = 128
NB = 4
FAN = 2
LIMIT = 16 << 20
BF16 = jnp.bfloat16
F32 = jnp.float32


def dot_t(a, b):
    return lax.dot_general(a, b, (((1,), (1,)), ((), ())), preferred_element_type=F32)


def div(a, b):
    return lax.div(a, jnp.int32(b))


def swaps(size, first, stride):
    pairs = []
    for i in range(size):
        block = i // stride
        other = i + stride if (block - first) % 2 == 0 else i - stride
        if 0 <= other < size:
            pairs.append((i, other))
    return pairs


def partner(d, first, stride):
    block = div(d, stride)
    return jnp.where((block - first) % 2 == 0, d + stride, d - stride)


def clip(i, size):
    return jnp.minimum(jnp.maximum(i, 0), size - 1)


class Tables:
    def __init__(self, lp, mp, lc, mc, nl, nm, nt):
        self.lp, self.mp, self.lc, self.mc = lp, mp, lc, mc
        self.nl, self.nm, self.nt = nl, nm, nt

    def leaf(self, s):
        s = clip(s, self.lp.shape[0])
        p = self.lp[s]
        code = self.lc[s]
        q = self.mp[p]
        return p, q, code

    def leaf_source(self, s):
        p, q, code = self.leaf(s)
        near = code < NB
        device = jnp.where(near, div(p, self.nm), div(q, self.nt))
        row = jnp.where(near, p - div(p, self.nm) * self.nm, q - div(q, self.nt) * self.nt)
        return near, device, row, jnp.where(near, code, code - NB)

    def mid_source(self, m):
        m = clip(m, self.mp.shape[0])
        q = self.mp[m]
        return div(q, self.nt), q - div(q, self.nt) * self.nt, self.mc[m]


def block_of(ref, row, blk):
    return ref[row, :, pl.ds(pl.multiple_of(blk * BLK, BLK), BLK)]


def leaf_pick(tabs, s, mprim, tprim):
    near, _, row, blk = tabs.leaf_source(s)
    a = block_of(mprim, jnp.where(near, row, 0), blk)
    b = block_of(tprim, jnp.where(near, 0, row), blk)
    return jnp.where(near, a, b)


def mid_pick(tabs, m, tprim):
    _, row, blk = tabs.mid_source(m)
    return block_of(tprim, row, blk)


def move(sems, pairs):
    copies = [pltpu.make_async_copy(*pair, sems.at[i]) for i, pair in enumerate(pairs)]
    for copy in copies:
        copy.start()
    return copies


def leaf_kernel(lp_h, mp_h, lc_h, mc_h, lv_h, mv_h, cot_h, inv_h, pan_h, mprim_h, tprim_h,
                later_a, later_b, later_c, later_d, later_e, lp, mp, lc, mc, lv, mv,
                adj, upd, send_z, send_y, far_a, far_b, mprim, tprim,
                out_a, out_b, out_c, out_d, out_e, cot, inv, pan, sems, table_sems):
    nl, nm, nt = cot.shape[0], mprim.shape[0], tprim.shape[0]
    tables = [(lp_h, lp), (mp_h, mp), (lc_h, lc), (mc_h, mc), (lv_h, lv), (mv_h, mv)]
    reads = move(table_sems, tables)
    pairs = [(mprim_h, mprim), (tprim_h, tprim), (cot_h, cot)]
    pairs += [(inv_h.at[s], inv.at[s]) for s in range(nl)]
    pairs += [(pan_h.at[s], pan.at[s]) for s in range(nl)]
    pairs += [(later_a, out_a), (later_b, out_b), (later_c, out_c), (later_d, out_d),
              (later_e, out_e)]
    copies = move(sems, pairs)
    d = lax.axis_index("leaf")
    tabs = Tables(lp, mp, lc, mc, nl, nm, nt)
    col = lax.broadcasted_iota(jnp.int32, upd.shape[1:], 1)
    for copy in reads + copies[:2]:
        copy.wait()
    for out, first in ((send_z, 1), (send_y, 0)):
        t = partner(d, first, 1)
        for i in range(nl):
            out[FAN + i] = leaf_pick(tabs, t * nl + i, mprim, tprim)
        for i in range(nm):
            out[FAN + nl + i] = mid_pick(tabs, t * nm + i, tprim)
    for out, first in ((far_a, 0), (far_b, 1)):
        t = partner(d, first, 2)
        start = jnp.where(t > d, 0, nl - FAN)
        for i in range(FAN):
            _, _, row, blk = tabs.leaf_source(t * nl + start + i)
            out[i] = block_of(tprim, jnp.minimum(row, nt - 1), blk)
    copies[2].wait()
    for s in range(nl):
        copies[3 + s].wait()
        adj[s] = dot_t(cot[s], inv[s]).astype(BF16)
    for s in range(nl):
        copies[3 + nl + s].wait()
    for s in range(nl):
        upd[s] = jnp.where(col < lv[s], dot_t(adj[s], pan[s]), 0.0)
    for out, first in ((send_z, 1), (send_y, 0)):
        start = jnp.where(partner(d, first, 1) > d, nl - FAN, 0)
        for i in range(FAN):
            out[i] = upd[start + i].astype(BF16)
    for copy in copies[3 + 2 * nl:]:
        copy.wait()


def mid_kernel(lp, mp, lc, mc, lv, mv, rec_z, rec_y, upd, cot, inv, pan,
               mprim, tprim, adj, rows, send_z, send_y, keep, acc):
    nl, nm, nt = upd.shape[0], mprim.shape[0], tprim.shape[0]
    d = lax.axis_index("leaf")
    tabs = Tables(lp, mp, lc, mc, nl, nm, nt)
    base = nm * NB
    dump = base + 3 * nt * NB
    for m in range(nm):
        for k in range(NB):
            acc[m * NB + k] = cot[m, :, k * BLK:(k + 1) * BLK].astype(F32)
    for k in range(base, dump):
        acc[k] = jnp.zeros(acc.shape[1:], F32)
    total = lp.shape[0]

    def top_slot(q, k):
        return clip(base + (q - (d - 1) * nt) * NB + k, dump)

    def take(s, value):
        p, q, code = tabs.leaf(s)
        mine = (s >= 0) & (s < total) & (div(p, nm) == d)
        slot = jnp.where(code < NB, (p - d * nm) * NB + code, top_slot(q, code - NB))
        slot = jnp.where(mine, clip(slot, dump), dump)
        acc[slot] = acc[slot] - value

    for i in range(nl):
        take(d * nl + i, upd[i])
    near = []
    for rec, first in ((rec_z, 1), (rec_y, 0)):
        t = partner(d, first, 1)
        near.append((t, rec))
        start = jnp.where(t > d, t * nl, (t + 1) * nl - FAN)
        for i in range(FAN):
            take(start + i, rec[i].astype(F32))
    col = lax.broadcasted_iota(jnp.int32, acc.shape[1:], 1)
    for m in range(nm):
        rhs = jnp.concatenate([acc[m * NB + k].astype(BF16) for k in range(NB)], axis=1)
        a = dot_t(rhs, inv[m]).astype(BF16)
        adj[m] = a
        u = jnp.where(col < mv[m], dot_t(a, pan[m]), 0.0)
        p = d * nm + m
        slot = top_slot(mp[p], mc[p])
        acc[slot] = acc[slot] - u
    for out, (t, _) in ((send_z, near[0]), (send_y, near[1])):
        for k in range(nt * NB):
            out[k] = acc[base + (t - d + 1) * nt * NB + k].astype(BF16)
    for k in range(nt * NB):
        keep[k] = acc[base + nt * NB + k]
    for i in range(nl):
        _, dev, _, _ = tabs.leaf_source(d * nl + i)
        value = leaf_pick(tabs, d * nl + i, mprim, tprim)
        for t, rec in near:
            value = jnp.where(dev == t, rec[FAN + i], value)
        rows[i] = jnp.where(col < lv[i], value, jnp.zeros_like(value))
    for i in range(nm):
        dev, _, _ = tabs.mid_source(d * nm + i)
        value = mid_pick(tabs, d * nm + i, tprim)
        for t, rec in near:
            value = jnp.where(dev == t, rec[FAN + nl + i], value)
        rows[nl + i] = jnp.where(col < mv[i], value, jnp.zeros_like(value))


def grad_kernel(groups, lp, mp, lc, mc, lv, mv, far_a, far_b, far_a_x, far_b_x, leaf_own,
                leaf_other, mid_own, mid_other, rows_own, rows_other, leaf_out, mid_out, keep_leaf, keep_mid, *rest):
    sends, cols, sems = rest[:-2], rest[-2], rest[-1]
    copies = [pltpu.make_async_copy(leaf_own, leaf_out, sems.at[0]),
              pltpu.make_async_copy(mid_own, mid_out, sems.at[1])]
    for copy in copies:
        copy.start()
    nl, nm = leaf_own.shape[0], mid_own.shape[0]
    d, j = lax.axis_index("leaf"), lax.axis_index("rhs")
    tabs = Tables(lp, mp, lc, mc, nl, nm, nm // FAN)
    col = lax.broadcasted_iota(jnp.int32, (FAN * rows_own.shape[1], BLK), 1)
    x = div(j, 2)
    far = ((partner(d, 0, 2), far_a, far_a_x), (partner(d, 1, 2), far_b, far_b_x))
    width = keep_leaf.shape[1]
    for s in range(rows_own.shape[0]):
        own, other, keep, i = leaf_own, leaf_other, keep_leaf, s
        if s >= nl:
            own, other, keep, i = mid_own, mid_other, keep_mid, s - nl
        both = jnp.concatenate([rows_own[s], rows_other[s]], axis=0)
        if s < nl:
            _, dev, _, _ = tabs.leaf_source(d * nl + s)
            for t, *recs in far:
                take = (dev == t) & (col < lv[s])
                if s < FAN:
                    value = jnp.concatenate([rec[s] for rec in recs], axis=0)
                    both = jnp.where(take & (t < d), value, both)
                if s >= nl - FAN:
                    value = jnp.concatenate([rec[s - nl + FAN] for rec in recs], axis=0)
                    both = jnp.where(take & (t > d), value, both)
        adj = jnp.concatenate([own[i], other[i]], axis=0)
        cols[s] = lax.dot_general(
            both, adj, (((0,), (0,)), ((), ())), preferred_element_type=F32
        )
        keep[i] = cols[s, pl.ds(pl.multiple_of(j * width, width), width), :]
        for step, out in enumerate(sends, 1):
            to = (x + step) % groups * 2 + j % 2
            out[s] = cols[s, pl.ds(pl.multiple_of(to * width, width), width), :].astype(BF16)
    for copy in copies:
        copy.wait()


def last_kernel(keep, rec_z, rec_y, cot, inv, leaf_sum, mid_sum, *rest):
    gets, (adj, leaf_out, mid_out) = rest[:-3], rest[-3:]
    nl = leaf_sum.shape[0]
    for total, out, first in ((leaf_sum, leaf_out, 0), (mid_sum, mid_out, nl)):
        for i in range(total.shape[0]):
            value = total[i]
            for get in gets:
                value = value + get[first + i].astype(F32)
            out[i] = (-value).astype(BF16)
    for q in range(cot.shape[0]):
        parts = []
        for k in range(NB):
            total = keep[q * NB + k] + rec_z[q * NB + k].astype(F32) + rec_y[q * NB + k].astype(F32)
            total = total + cot[q, :, k * BLK:(k + 1) * BLK].astype(F32)
            parts.append(total.astype(BF16))
        adj[q] = dot_t(jnp.concatenate(parts, axis=1), inv[q]).astype(BF16)


SPEC = {m: pl.BlockSpec(memory_space=m) for m in (pltpu.SMEM, pltpu.VMEM, pltpu.HBM)}
DMA = pltpu.SemaphoreType.DMA


def call(kernel, tables, far, near, outs, scratch=()):
    operands, places = [], []
    for values, place in ((tables, pltpu.SMEM), (far, pltpu.HBM), (near, pltpu.VMEM)):
        operands += [pltpu.with_memory_space_constraint(v, place) for v in values]
        places += [SPEC[place]] * len(values)
    shapes = []
    for shape, dtype, place in outs:
        shapes.append(place(shape, dtype) if place else jax.ShapeDtypeStruct(shape, dtype))
    return pl.pallas_call(
        kernel,
        out_shape=shapes,
        in_specs=places,
        out_specs=[SPEC[place or pltpu.VMEM] for _, _, place in outs],
        scratch_shapes=list(scratch),
        compiler_params=pltpu.CompilerParams(vmem_limit_bytes=LIMIT),
    )(*operands)


def shards(leaf_parents, mid_parents, leaf_codes, mid_codes, leaf_valid, mid_valid,
           leaf_inverse, mid_inverse, top_inverse, leaf_panels, mid_panels,
           leaf_cotangent, mid_cotangent, top_cotangent, mid_primal, top_primal):
    nl, probes, width = leaf_cotangent.shape
    nm = mid_cotangent.shape[0]
    nt = top_cotangent.shape[0]
    rows = leaf_panels.shape[1]
    leaves = lax.axis_size("leaf")
    peers = lax.axis_size("rhs")
    groups = peers // 2
    assert leaf_codes.shape[1] == 1 and mid_codes.shape[1] == 1 and rows == BLK
    tables = (leaf_parents, mid_parents, leaf_codes.reshape(-1), mid_codes.reshape(-1),
              leaf_valid, mid_valid)
    load = FAN + nl + nm

    def along(value, first, stride):
        return lax.ppermute(value, "leaf", swaps(leaves, first, stride))

    def core_swap(value):
        return lax.ppermute(value, "rhs", [(i, i ^ 1) for i in range(peers)])

    def near(shape, dtype):
        return (shape, dtype, pltpu.VMEM)

    def same(value):
        return near(value.shape, value.dtype)

    piece = (probes, BLK)
    moved = (mid_primal, top_primal, mid_cotangent, mid_inverse, mid_panels, top_cotangent,
             top_inverse)
    (*tables, leaf_adj, upd, send_z, send_y, far_a, far_b, mprim, tprim, mid_cot, mid_inv, mid_pan,
     top_cot, top_inv) = call(
        leaf_kernel, (),
        (*tables, leaf_cotangent, leaf_inverse, leaf_panels, *moved), (),
        [*((t.shape, t.dtype, pltpu.SMEM) for t in tables),
         near((nl, probes, width), BF16), near((nl, *piece), F32), near((load, *piece), BF16),
         near((load, *piece), BF16), near((FAN, *piece), BF16), near((FAN, *piece), BF16),
         *map(same, moved)],
        [pltpu.VMEM(v.shape, v.dtype) for v in (leaf_cotangent, leaf_inverse, leaf_panels)]
        + [DMA((1 + 2 * nl + len(moved),)), DMA((len(tables),))],
    )
    rec_z = along(send_z, 1, 1)
    rec_y = along(send_y, 0, 1)
    far_a = along(far_a, 0, 2)
    far_b = along(far_b, 1, 2)
    leaf_other = core_swap(leaf_adj)
    mid_adj, row_blocks, send_z, send_y, keep = call(
        mid_kernel, tables, (),
        (rec_z, rec_y, upd, mid_cot, mid_inv, mid_pan, mprim, tprim),
        [near((nm, probes, width), BF16), near((nl + nm, *piece), BF16),
         near((nt * NB, *piece), BF16), near((nt * NB, *piece), BF16),
         near((nt * NB, *piece), F32)],
        [pltpu.VMEM((nm * NB + 3 * nt * NB + 1, *piece), F32)],
    )
    rec_z = along(send_z, 1, 1)
    rec_y = along(send_y, 0, 1)
    mid_other = core_swap(mid_adj)
    rows_other = core_swap(row_blocks)
    far_a_x = core_swap(far_a)
    far_b_x = core_swap(far_b)
    part = (rows // peers, width)
    leaf_out, mid_out, leaf_sum, mid_sum, *sends = call(
        lambda *refs: grad_kernel(groups, *refs), tables, (),
        (far_a, far_b, far_a_x, far_b_x, leaf_adj, leaf_other, mid_adj, mid_other, row_blocks, rows_other),
        [((nl, probes, width), BF16, pltpu.HBM), ((nm, probes, width), BF16, pltpu.HBM),
         near((nl, *part), F32), near((nm, *part), F32)]
        + [near((nl + nm, *part), BF16)] * (groups - 1),
        [pltpu.VMEM((nl + nm, rows, width), F32), DMA((2,))],
    )
    gets = []
    for step, value in enumerate(sends, 1):
        pairs = [(i, (i // 2 + step) % groups * 2 + i % 2) for i in range(peers)]
        gets.append(lax.ppermute(value, "rhs", pairs))
    top_adj, leaf_grad, mid_grad = call(
        last_kernel, (), (),
        (keep, rec_z, rec_y, top_cot, top_inv, leaf_sum, mid_sum, *gets),
        [((nt, probes, width), BF16, None), ((nl, *part), BF16, None), ((nm, *part), BF16, None)],
    )
    return leaf_out, mid_out, top_adj, leaf_grad, mid_grad


def solution(mesh):
    each = P("leaf")
    block = P("leaf", None, None)
    split = P("leaf", "rhs", None)

    return jax.shard_map(
        shards,
        mesh=mesh,
        in_specs=(P(),) * 4 + (each,) * 2 + (block,) * 5 + (split,) * 5,
        out_specs=(split,) * 5,
        check_vma=False,
    )
```

```python
import jax
import jax.numpy as jnp
from jax import lax
from jax.experimental import pallas as pl
from jax.experimental.pallas import tpu as pltpu
from jax.sharding import PartitionSpec as P


BLK = 128
NB = 4
FAN = 2
LIMIT = 16 << 20
BF16 = jnp.bfloat16
F32 = jnp.float32


def dot_t(a, b):
    return lax.dot_general(a, b, (((1,), (1,)), ((), ())), preferred_element_type=F32)


def div(a, b):
    return lax.div(a, jnp.int32(b))


def swaps(size, first, stride):
    pairs = []
    for i in range(size):
        block = i // stride
        other = i + stride if (block - first) % 2 == 0 else i - stride
        if 0 <= other < size:
            pairs.append((i, other))
    return pairs


def partner(d, first, stride):
    block = div(d, stride)
    return jnp.where((block - first) % 2 == 0, d + stride, d - stride)


def clip(i, size):
    return jnp.minimum(jnp.maximum(i, 0), size - 1)


class Tables:
    def __init__(self, lp, mp, lc, mc, nl, nm, nt):
        self.lp, self.mp, self.lc, self.mc = lp, mp, lc, mc
        self.nl, self.nm, self.nt = nl, nm, nt

    def leaf(self, s):
        s = clip(s, self.lp.shape[0])
        p = self.lp[s]
        code = self.lc[s]
        q = self.mp[p]
        return p, q, code

    def leaf_source(self, s):
        p, q, code = self.leaf(s)
        near = code < NB
        device = jnp.where(near, div(p, self.nm), div(q, self.nt))
        row = jnp.where(near, p - div(p, self.nm) * self.nm, q - div(q, self.nt) * self.nt)
        return near, device, row, jnp.where(near, code, code - NB)

    def mid_source(self, m):
        m = clip(m, self.mp.shape[0])
        q = self.mp[m]
        return div(q, self.nt), q - div(q, self.nt) * self.nt, self.mc[m]


def block_of(ref, row, blk):
    return ref[row, :, pl.ds(pl.multiple_of(blk * BLK, BLK), BLK)]


def leaf_pick(tabs, s, mprim, tprim):
    near, _, row, blk = tabs.leaf_source(s)
    a = block_of(mprim, jnp.where(near, row, 0), blk)
    b = block_of(tprim, jnp.where(near, 0, row), blk)
    return jnp.where(near, a, b)


def mid_pick(tabs, m, tprim):
    _, row, blk = tabs.mid_source(m)
    return block_of(tprim, row, blk)


def move(sems, pairs):
    copies = [pltpu.make_async_copy(*pair, sems.at[i]) for i, pair in enumerate(pairs)]
    for copy in copies:
        copy.start()
    return copies


def leaf_kernel(lp_h, mp_h, lc_h, mc_h, lv_h, mv_h, cot_h, inv_h, pan_h, mprim_h, tprim_h,
                later_a, later_b, later_c, later_d, later_e, lp, mp, lc, mc, lv, mv,
                adj, upd, send_z, send_y, mprim, tprim,
                out_a, out_b, out_c, out_d, out_e, cot, inv, pan, sems, table_sems):
    nl, nm, nt = cot.shape[0], mprim.shape[0], tprim.shape[0]
    tables = [(lp_h, lp), (mp_h, mp), (lc_h, lc), (mc_h, mc), (lv_h, lv), (mv_h, mv)]
    reads = move(table_sems, tables)
    pairs = [(mprim_h, mprim), (tprim_h, tprim), (cot_h, cot)]
    pairs += [(inv_h.at[s], inv.at[s]) for s in range(nl)]
    pairs += [(pan_h.at[s], pan.at[s]) for s in range(nl)]
    pairs += [(later_a, out_a), (later_b, out_b), (later_c, out_c), (later_d, out_d),
              (later_e, out_e)]
    copies = move(sems, pairs)
    d = lax.axis_index("leaf")
    tabs = Tables(lp, mp, lc, mc, nl, nm, nt)
    col = lax.broadcasted_iota(jnp.int32, upd.shape[1:], 1)

    def picks(out, first):
        t = partner(d, first, 1)
        for i in range(nl):
            out[FAN + i] = leaf_pick(tabs, t * nl + i, mprim, tprim)
        for i in range(nm):
            out[FAN + nl + i] = mid_pick(tabs, t * nm + i, tprim)

    for copy in reads + copies[:2]:
        copy.wait()
    picks(send_z, 1)
    picks(send_y, 0)
    for copy in copies[2:3 + nl // 2]:
        copy.wait()
    for s in range(nl // 2):
        adj[s] = dot_t(cot[s], inv[s]).astype(BF16)
    for copy in copies[3 + nl // 2:3 + 2 * nl]:
        copy.wait()
    for s in range(nl // 2, nl):
        adj[s] = dot_t(cot[s], inv[s]).astype(BF16)
    for s in range(nl):
        upd[s] = jnp.where(col < lv[s], dot_t(adj[s], pan[s]), 0.0)
    for out, first in ((send_z, 1), (send_y, 0)):
        start = jnp.where(partner(d, first, 1) > d, nl - FAN, 0)
        for i in range(FAN):
            out[i] = upd[start + i].astype(BF16)
    for copy in copies[3 + 2 * nl:]:
        copy.wait()


def far_kernel(nl, nm, lp, mp, lc, mc, lv, mv, tprim, tprim_x, far_a, far_b):
    nt = tprim.shape[0]
    probes = tprim.shape[1]
    d = lax.axis_index("leaf")
    tabs = Tables(lp, mp, lc, mc, nl, nm, nt)
    for out, first in ((far_a, 0), (far_b, 1)):
        t = partner(d, first, 2)
        start = jnp.where(t > d, 0, nl - FAN)
        for i in range(FAN):
            _, _, row, blk = tabs.leaf_source(t * nl + start + i)
            row = jnp.minimum(row, nt - 1)
            out[i, :probes] = block_of(tprim, row, blk)
            out[i, probes:] = block_of(tprim_x, row, blk)


def mid_kernel(lp, mp, lc, mc, lv, mv, rec_z, rec_y, upd, cot, inv, pan,
               mprim, tprim, adj, rows, send_z, send_y, keep, acc):
    nl, nm, nt = upd.shape[0], mprim.shape[0], tprim.shape[0]
    d = lax.axis_index("leaf")
    tabs = Tables(lp, mp, lc, mc, nl, nm, nt)
    base = nm * NB
    dump = base + 3 * nt * NB
    for m in range(nm):
        for k in range(NB):
            acc[m * NB + k] = cot[m, :, k * BLK:(k + 1) * BLK].astype(F32)
    for k in range(base, dump):
        acc[k] = jnp.zeros(acc.shape[1:], F32)
    total = lp.shape[0]

    def top_slot(q, k):
        return clip(base + (q - (d - 1) * nt) * NB + k, dump)

    def take(s, value):
        p, q, code = tabs.leaf(s)
        mine = (s >= 0) & (s < total) & (div(p, nm) == d)
        slot = jnp.where(code < NB, (p - d * nm) * NB + code, top_slot(q, code - NB))
        slot = jnp.where(mine, clip(slot, dump), dump)
        acc[slot] = acc[slot] - value

    for i in range(nl):
        take(d * nl + i, upd[i])
    near = []
    for rec, first in ((rec_z, 1), (rec_y, 0)):
        t = partner(d, first, 1)
        near.append((t, rec))
        start = jnp.where(t > d, t * nl, (t + 1) * nl - FAN)
        for i in range(FAN):
            take(start + i, rec[i].astype(F32))
    col = lax.broadcasted_iota(jnp.int32, acc.shape[1:], 1)
    for m in range(nm):
        rhs = jnp.concatenate([acc[m * NB + k].astype(BF16) for k in range(NB)], axis=1)
        a = dot_t(rhs, inv[m]).astype(BF16)
        adj[m] = a
        u = jnp.where(col < mv[m], dot_t(a, pan[m]), 0.0)
        p = d * nm + m
        slot = top_slot(mp[p], mc[p])
        acc[slot] = acc[slot] - u
    for out, (t, _) in ((send_z, near[0]), (send_y, near[1])):
        for k in range(nt * NB):
            out[k] = acc[base + (t - d + 1) * nt * NB + k].astype(BF16)
    for k in range(nt * NB):
        keep[k] = acc[base + nt * NB + k]
    for i in range(nl):
        _, dev, _, _ = tabs.leaf_source(d * nl + i)
        value = leaf_pick(tabs, d * nl + i, mprim, tprim)
        for t, rec in near:
            value = jnp.where(dev == t, rec[FAN + i], value)
        rows[i] = jnp.where(col < lv[i], value, jnp.zeros_like(value))
    for i in range(nm):
        dev, _, _ = tabs.mid_source(d * nm + i)
        value = mid_pick(tabs, d * nm + i, tprim)
        for t, rec in near:
            value = jnp.where(dev == t, rec[FAN + nl + i], value)
        rows[nl + i] = jnp.where(col < mv[i], value, jnp.zeros_like(value))


def grad_kernel(groups, lp, mp, lc, mc, lv, mv, far_a, far_b, leaf_own,
                leaf_other, mid_own, mid_other, rows_own, rows_other, leaf_out, mid_out, keep_leaf, keep_mid, *rest):
    sends, cols, sems = rest[:-2], rest[-2], rest[-1]
    copies = [pltpu.make_async_copy(leaf_own, leaf_out, sems.at[0]),
              pltpu.make_async_copy(mid_own, mid_out, sems.at[1])]
    for copy in copies:
        copy.start()
    nl, nm = leaf_own.shape[0], mid_own.shape[0]
    d, j = lax.axis_index("leaf"), lax.axis_index("rhs")
    tabs = Tables(lp, mp, lc, mc, nl, nm, nm // FAN)
    col = lax.broadcasted_iota(jnp.int32, (FAN * rows_own.shape[1], BLK), 1)
    x = div(j, 2)
    far = ((partner(d, 0, 2), far_a), (partner(d, 1, 2), far_b))
    width = keep_leaf.shape[1]
    for s in range(rows_own.shape[0]):
        own, other, keep, i = leaf_own, leaf_other, keep_leaf, s
        if s >= nl:
            own, other, keep, i = mid_own, mid_other, keep_mid, s - nl
        both = jnp.concatenate([rows_own[s], rows_other[s]], axis=0)
        if s < nl:
            _, dev, _, _ = tabs.leaf_source(d * nl + s)
            for t, rec in far:
                take = (dev == t) & (col < lv[s])
                if s < FAN:
                    both = jnp.where(take & (t < d), rec[s], both)
                if s >= nl - FAN:
                    both = jnp.where(take & (t > d), rec[s - nl + FAN], both)
        adj = jnp.concatenate([own[i], other[i]], axis=0)
        cols[s] = lax.dot_general(
            both, adj, (((0,), (0,)), ((), ())), preferred_element_type=F32
        )
        keep[i] = cols[s, pl.ds(pl.multiple_of(j * width, width), width), :]
        for step, out in enumerate(sends, 1):
            to = (x + step) % groups * 2 + j % 2
            out[s] = cols[s, pl.ds(pl.multiple_of(to * width, width), width), :].astype(BF16)
    for copy in copies:
        copy.wait()


def last_kernel(keep, rec_z, rec_y, cot, inv, leaf_sum, mid_sum, *rest):
    gets, (adj, leaf_out, mid_out) = rest[:-3], rest[-3:]
    nl = leaf_sum.shape[0]
    for total, out, first in ((leaf_sum, leaf_out, 0), (mid_sum, mid_out, nl)):
        for i in range(total.shape[0]):
            value = total[i]
            for get in gets:
                value = value + get[first + i].astype(F32)
            out[i] = (-value).astype(BF16)
    for q in range(cot.shape[0]):
        parts = []
        for k in range(NB):
            total = keep[q * NB + k] + rec_z[q * NB + k].astype(F32) + rec_y[q * NB + k].astype(F32)
            total = total + cot[q, :, k * BLK:(k + 1) * BLK].astype(F32)
            parts.append(total.astype(BF16))
        adj[q] = dot_t(jnp.concatenate(parts, axis=1), inv[q]).astype(BF16)


SPEC = {m: pl.BlockSpec(memory_space=m) for m in (pltpu.SMEM, pltpu.VMEM, pltpu.HBM)}
DMA = pltpu.SemaphoreType.DMA


def call(kernel, tables, far, near, outs, scratch=()):
    operands, places = [], []
    for values, place in ((tables, pltpu.SMEM), (far, pltpu.HBM), (near, pltpu.VMEM)):
        operands += [pltpu.with_memory_space_constraint(v, place) for v in values]
        places += [SPEC[place]] * len(values)
    shapes = []
    for shape, dtype, place in outs:
        shapes.append(place(shape, dtype) if place else jax.ShapeDtypeStruct(shape, dtype))
    return pl.pallas_call(
        kernel,
        out_shape=shapes,
        in_specs=places,
        out_specs=[SPEC[place or pltpu.VMEM] for _, _, place in outs],
        scratch_shapes=list(scratch),
        compiler_params=pltpu.CompilerParams(vmem_limit_bytes=LIMIT),
    )(*operands)


def shards(leaf_parents, mid_parents, leaf_codes, mid_codes, leaf_valid, mid_valid,
           leaf_inverse, mid_inverse, top_inverse, leaf_panels, mid_panels,
           leaf_cotangent, mid_cotangent, top_cotangent, mid_primal, top_primal):
    nl, probes, width = leaf_cotangent.shape
    nm = mid_cotangent.shape[0]
    nt = top_cotangent.shape[0]
    rows = leaf_panels.shape[1]
    leaves = lax.axis_size("leaf")
    peers = lax.axis_size("rhs")
    groups = peers // 2
    assert leaf_codes.shape[1] == 1 and mid_codes.shape[1] == 1 and rows == BLK
    tables = (leaf_parents, mid_parents, leaf_codes.reshape(-1), mid_codes.reshape(-1),
              leaf_valid, mid_valid)
    load = FAN + nl + nm

    def along(value, first, stride):
        return lax.ppermute(value, "leaf", swaps(leaves, first, stride))

    def core_swap(value):
        return lax.ppermute(value, "rhs", [(i, i ^ 1) for i in range(peers)])

    def near(shape, dtype):
        return (shape, dtype, pltpu.VMEM)

    def same(value):
        return near(value.shape, value.dtype)

    piece = (probes, BLK)
    tprim_x = core_swap(top_primal)
    moved = (mid_primal, top_primal, mid_cotangent, mid_inverse, mid_panels, top_cotangent,
             top_inverse)
    (*tables, leaf_adj, upd, send_z, send_y, mprim, tprim, mid_cot, mid_inv, mid_pan,
     top_cot, top_inv) = call(
        leaf_kernel, (),
        (*tables, leaf_cotangent, leaf_inverse, leaf_panels, *moved), (),
        [*((t.shape, t.dtype, pltpu.SMEM) for t in tables),
         near((nl, probes, width), BF16), near((nl, *piece), F32), near((load, *piece), BF16),
         near((load, *piece), BF16), *map(same, moved)],
        [pltpu.VMEM(v.shape, v.dtype) for v in (leaf_cotangent, leaf_inverse, leaf_panels)]
        + [DMA((1 + 2 * nl + len(moved),)), DMA((len(tables),))],
    )
    rec_z = along(send_z, 1, 1)
    rec_y = along(send_y, 0, 1)
    far_a, far_b = call(
        lambda *refs: far_kernel(nl, nm, *refs), tables, (), (tprim, tprim_x),
        [near((FAN, 2 * probes, BLK), BF16)] * 2,
    )
    far_a = along(far_a, 0, 2)
    far_b = along(far_b, 1, 2)
    leaf_other = core_swap(leaf_adj)
    mid_adj, row_blocks, send_z, send_y, keep = call(
        mid_kernel, tables, (),
        (rec_z, rec_y, upd, mid_cot, mid_inv, mid_pan, mprim, tprim),
        [near((nm, probes, width), BF16), near((nl + nm, *piece), BF16),
         near((nt * NB, *piece), BF16), near((nt * NB, *piece), BF16),
         near((nt * NB, *piece), F32)],
        [pltpu.VMEM((nm * NB + 3 * nt * NB + 1, *piece), F32)],
    )
    rec_z = along(send_z, 1, 1)
    rec_y = along(send_y, 0, 1)
    mid_other = core_swap(mid_adj)
    rows_other = core_swap(row_blocks)
    part = (rows // peers, width)
    leaf_out, mid_out, leaf_sum, mid_sum, *sends = call(
        lambda *refs: grad_kernel(groups, *refs), tables, (),
        (far_a, far_b, leaf_adj, leaf_other, mid_adj, mid_other, row_blocks, rows_other),
        [((nl, probes, width), BF16, pltpu.HBM), ((nm, probes, width), BF16, pltpu.HBM),
         near((nl, *part), F32), near((nm, *part), F32)]
        + [near((nl + nm, *part), BF16)] * (groups - 1),
        [pltpu.VMEM((nl + nm, rows, width), F32), DMA((2,))],
    )
    gets = []
    for step, value in enumerate(sends, 1):
        pairs = [(i, (i // 2 + step) % groups * 2 + i % 2) for i in range(peers)]
        gets.append(lax.ppermute(value, "rhs", pairs))
    top_adj, leaf_grad, mid_grad = call(
        last_kernel, (), (),
        (keep, rec_z, rec_y, top_cot, top_inv, leaf_sum, mid_sum, *gets),
        [((nt, probes, width), BF16, None), ((nl, *part), BF16, None), ((nm, *part), BF16, None)],
    )
    return leaf_out, mid_out, top_adj, leaf_grad, mid_grad


def solution(mesh):
    each = P("leaf")
    block = P("leaf", None, None)
    split = P("leaf", "rhs", None)

    return jax.shard_map(
        shards,
        mesh=mesh,
        in_specs=(P(),) * 4 + (each,) * 2 + (block,) * 5 + (split,) * 5,
        out_specs=(split,) * 5,
        check_vma=False,
    )
```

```python
import jax
import jax.numpy as jnp
from jax import lax
from jax.experimental import pallas as pl
from jax.experimental.pallas import tpu as pltpu
from jax.sharding import PartitionSpec as P


BLK = 128
NB = 4
FAN = 2
LIMIT = 16 << 20
BF16 = jnp.bfloat16
F32 = jnp.float32


def dot_t(a, b):
    return lax.dot_general(a, b, (((1,), (1,)), ((), ())), preferred_element_type=F32)


def div(a, b):
    return lax.div(a, jnp.int32(b))


def swaps(size, first, stride):
    pairs = []
    for i in range(size):
        block = i // stride
        other = i + stride if (block - first) % 2 == 0 else i - stride
        if 0 <= other < size:
            pairs.append((i, other))
    return pairs


def partner(d, first, stride):
    block = div(d, stride)
    return jnp.where((block - first) % 2 == 0, d + stride, d - stride)


def clip(i, size):
    return jnp.minimum(jnp.maximum(i, 0), size - 1)


class Tables:
    def __init__(self, lp, mp, lc, mc, nl, nm, nt):
        self.lp, self.mp, self.lc, self.mc = lp, mp, lc, mc
        self.nl, self.nm, self.nt = nl, nm, nt

    def leaf(self, s):
        s = clip(s, self.lp.shape[0])
        p = self.lp[s]
        code = self.lc[s]
        q = self.mp[p]
        return p, q, code

    def leaf_source(self, s):
        p, q, code = self.leaf(s)
        near = code < NB
        device = jnp.where(near, div(p, self.nm), div(q, self.nt))
        row = jnp.where(near, p - div(p, self.nm) * self.nm, q - div(q, self.nt) * self.nt)
        return near, device, row, jnp.where(near, code, code - NB)

    def mid_source(self, m):
        m = clip(m, self.mp.shape[0])
        q = self.mp[m]
        return div(q, self.nt), q - div(q, self.nt) * self.nt, self.mc[m]


def block_of(ref, row, blk):
    return ref[row, :, pl.ds(pl.multiple_of(blk * BLK, BLK), BLK)]


def leaf_pick(tabs, s, mprim, tprim):
    near, _, row, blk = tabs.leaf_source(s)
    a = block_of(mprim, jnp.where(near, row, 0), blk)
    b = block_of(tprim, jnp.where(near, 0, row), blk)
    return jnp.where(near, a, b)


def mid_pick(tabs, m, tprim):
    _, row, blk = tabs.mid_source(m)
    return block_of(tprim, row, blk)


def move(sems, pairs):
    copies = [pltpu.make_async_copy(*pair, sems.at[i]) for i, pair in enumerate(pairs)]
    for copy in copies:
        copy.start()
    return copies


def leaf_kernel(lp_h, mp_h, lc_h, mc_h, lv_h, mv_h, cot_h, inv_h, pan_h, mprim_h, tprim_h,
                later_a, later_b, later_c, later_d, later_e, lp, mp, lc, mc, lv, mv,
                adj, upd, send_z, send_y, mprim, tprim,
                out_a, out_b, out_c, out_d, out_e, cot, inv, pan, sems, table_sems):
    nl, nm, nt = cot.shape[0], mprim.shape[0], tprim.shape[0]
    tables = [(lp_h, lp), (mp_h, mp), (lc_h, lc), (mc_h, mc), (lv_h, lv), (mv_h, mv)]
    reads = move(table_sems, tables)
    pairs = [(mprim_h, mprim), (tprim_h, tprim), (cot_h, cot)]
    pairs += [(inv_h.at[s], inv.at[s]) for s in range(nl)]
    pairs += [(pan_h.at[s], pan.at[s]) for s in range(nl)]
    pairs += [(later_a, out_a), (later_b, out_b), (later_c, out_c), (later_d, out_d),
              (later_e, out_e)]
    copies = move(sems, pairs)
    d = lax.axis_index("leaf")
    tabs = Tables(lp, mp, lc, mc, nl, nm, nt)
    col = lax.broadcasted_iota(jnp.int32, upd.shape[1:], 1)

    def picks(out, first):
        t = partner(d, first, 1)
        for i in range(nl):
            out[FAN + i] = leaf_pick(tabs, t * nl + i, mprim, tprim)
        for i in range(nm):
            out[FAN + nl + i] = mid_pick(tabs, t * nm + i, tprim)

    for copy in reads + copies[:2]:
        copy.wait()
    picks(send_z, 1)
    picks(send_y, 0)
    for copy in copies[2:3 + nl // 2]:
        copy.wait()
    for s in range(nl // 2):
        adj[s] = dot_t(cot[s], inv[s]).astype(BF16)
    for copy in copies[3 + nl // 2:3 + 2 * nl]:
        copy.wait()
    for s in range(nl // 2, nl):
        adj[s] = dot_t(cot[s], inv[s]).astype(BF16)
    for s in range(nl):
        upd[s] = jnp.where(col < lv[s], dot_t(adj[s], pan[s]), 0.0)
    for out, first in ((send_z, 1), (send_y, 0)):
        start = jnp.where(partner(d, first, 1) > d, nl - FAN, 0)
        for i in range(FAN):
            out[i] = upd[start + i].astype(BF16)
    for copy in copies[3 + 2 * nl:]:
        copy.wait()


def far_kernel(nl, nm, lp, mp, lc, mc, lv, mv, tprim, tprim_x, far_a, far_b):
    nt = tprim.shape[0]
    probes = tprim.shape[1]
    d = lax.axis_index("leaf")
    tabs = Tables(lp, mp, lc, mc, nl, nm, nt)
    for out, first in ((far_a, 0), (far_b, 1)):
        t = partner(d, first, 2)
        start = jnp.where(t > d, 0, nl - FAN)
        for i in range(FAN):
            _, _, row, blk = tabs.leaf_source(t * nl + start + i)
            row = jnp.minimum(row, nt - 1)
            out[i, :probes] = block_of(tprim, row, blk)
            out[i, probes:] = block_of(tprim_x, row, blk)


def mid_kernel(lp, mp, lc, mc, lv, mv, rec_z, rec_y, upd, cot, inv, pan,
               mprim, tprim, adj, pack, send_z, send_y, keep, acc):
    nl, nm, nt = upd.shape[0], mprim.shape[0], tprim.shape[0]
    d = lax.axis_index("leaf")
    tabs = Tables(lp, mp, lc, mc, nl, nm, nt)
    base = nm * NB
    dump = base + 3 * nt * NB
    for m in range(nm):
        for k in range(NB):
            acc[m * NB + k] = cot[m, :, k * BLK:(k + 1) * BLK].astype(F32)
    for k in range(base, dump):
        acc[k] = jnp.zeros(acc.shape[1:], F32)
    total = lp.shape[0]

    def top_slot(q, k):
        return clip(base + (q - (d - 1) * nt) * NB + k, dump)

    def take(s, value):
        p, q, code = tabs.leaf(s)
        mine = (s >= 0) & (s < total) & (div(p, nm) == d)
        slot = jnp.where(code < NB, (p - d * nm) * NB + code, top_slot(q, code - NB))
        slot = jnp.where(mine, clip(slot, dump), dump)
        acc[slot] = acc[slot] - value

    for i in range(nl):
        take(d * nl + i, upd[i])
    near = []
    for rec, first in ((rec_z, 1), (rec_y, 0)):
        t = partner(d, first, 1)
        near.append((t, rec))
        start = jnp.where(t > d, t * nl, (t + 1) * nl - FAN)
        for i in range(FAN):
            take(start + i, rec[i].astype(F32))
    col = lax.broadcasted_iota(jnp.int32, acc.shape[1:], 1)
    for m in range(nm):
        rhs = jnp.concatenate([acc[m * NB + k].astype(BF16) for k in range(NB)], axis=1)
        a = dot_t(rhs, inv[m]).astype(BF16)
        adj[m] = a
        for k in range(NB):
            pack[nl + nm + m * NB + k] = a[:, k * BLK:(k + 1) * BLK]
        u = jnp.where(col < mv[m], dot_t(a, pan[m]), 0.0)
        p = d * nm + m
        slot = top_slot(mp[p], mc[p])
        acc[slot] = acc[slot] - u
    for out, (t, _) in ((send_z, near[0]), (send_y, near[1])):
        for k in range(nt * NB):
            out[k] = acc[base + (t - d + 1) * nt * NB + k].astype(BF16)
    for k in range(nt * NB):
        keep[k] = acc[base + nt * NB + k]
    for i in range(nl):
        _, dev, _, _ = tabs.leaf_source(d * nl + i)
        value = leaf_pick(tabs, d * nl + i, mprim, tprim)
        for t, rec in near:
            value = jnp.where(dev == t, rec[FAN + i], value)
        pack[i] = jnp.where(col < lv[i], value, jnp.zeros_like(value))
    for i in range(nm):
        dev, _, _ = tabs.mid_source(d * nm + i)
        value = mid_pick(tabs, d * nm + i, tprim)
        for t, rec in near:
            value = jnp.where(dev == t, rec[FAN + nl + i], value)
        pack[nl + i] = jnp.where(col < mv[i], value, jnp.zeros_like(value))


def grad_kernel(groups, lp, mp, lc, mc, lv, mv, far_a, far_b, leaf_own, leaf_other,
                rows_own, rows_other, keep_leaf, keep_mid, *rest):
    sends, cols = rest[:-1], rest[-1]
    nl, nm = leaf_own.shape[0], keep_mid.shape[0]
    d, j = lax.axis_index("leaf"), lax.axis_index("rhs")
    tabs = Tables(lp, mp, lc, mc, nl, nm, nm // FAN)
    both_probes = FAN * rows_own.shape[1]
    col = lax.broadcasted_iota(jnp.int32, (both_probes, BLK), 1)
    unit = (lax.broadcasted_iota(jnp.int32, (both_probes, both_probes), 0)
            == lax.broadcasted_iota(jnp.int32, (both_probes, both_probes), 1))
    unit = unit.astype(F32).astype(BF16)
    x = div(j, 2)
    far = ((partner(d, 0, 2), far_a), (partner(d, 1, 2), far_b))
    width = keep_leaf.shape[1]
    for s in range(nl + nm):
        both = jnp.concatenate([rows_own[s], rows_other[s]], axis=0)
        if s < nl:
            _, dev, _, _ = tabs.leaf_source(d * nl + s)
            for t, rec in far:
                take = (dev == t) & (col < lv[s])
                if s < FAN:
                    both = jnp.where(take & (t < d), rec[s], both)
                if s >= nl - FAN:
                    both = jnp.where(take & (t > d), rec[s - nl + FAN], both)
        cols[s] = lax.dot_general(
            both, unit, (((0,), (0,)), ((), ())), preferred_element_type=F32
        )
    for s in range(nl + nm):
        keep, i = (keep_leaf, s) if s < nl else (keep_mid, s - nl)
        if s < nl:
            adj = jnp.concatenate([leaf_own[s], leaf_other[s]], axis=0)
        else:
            blocks = [nl + nm + i * NB + k for k in range(NB)]
            adj = jnp.concatenate([jnp.concatenate([ref[b] for b in blocks], axis=1)
                                   for ref in (rows_own, rows_other)], axis=0)
        picked = [cols[s, pl.ds(pl.multiple_of(j * width, width), width), :]]
        for step in range(1, groups):
            to = (x + step) % groups * 2 + j % 2
            picked.append(cols[s, pl.ds(pl.multiple_of(to * width, width), width), :])
        value = lax.dot_general(
            jnp.concatenate(picked, axis=0).astype(BF16), adj, (((1,), (0,)), ((), ())),
            preferred_element_type=F32,
        )
        keep[i] = value[:width]
        for step, out in enumerate(sends, 1):
            out[s] = value[step * width:(step + 1) * width].astype(BF16)


def out_kernel(*refs):
    refs, sems = refs[:-1], refs[-1]
    half = len(refs) // 2
    for copy in move(sems, list(zip(refs[:half], refs[half:]))):
        copy.wait()


def last_kernel(keep, rec_z, rec_y, cot, inv, leaf_sum, mid_sum, *rest):
    gets, (adj, leaf_out, mid_out) = rest[:-3], rest[-3:]
    nl = leaf_sum.shape[0]
    for total, out, first in ((leaf_sum, leaf_out, 0), (mid_sum, mid_out, nl)):
        for i in range(total.shape[0]):
            value = total[i]
            for get in gets:
                value = value + get[first + i].astype(F32)
            out[i] = (-value).astype(BF16)
    for q in range(cot.shape[0]):
        parts = []
        for k in range(NB):
            total = keep[q * NB + k] + rec_z[q * NB + k].astype(F32) + rec_y[q * NB + k].astype(F32)
            total = total + cot[q, :, k * BLK:(k + 1) * BLK].astype(F32)
            parts.append(total.astype(BF16))
        adj[q] = dot_t(jnp.concatenate(parts, axis=1), inv[q]).astype(BF16)


SPEC = {m: pl.BlockSpec(memory_space=m) for m in (pltpu.SMEM, pltpu.VMEM, pltpu.HBM)}
DMA = pltpu.SemaphoreType.DMA


def call(kernel, tables, far, near, outs, scratch=()):
    operands, places = [], []
    for values, place in ((tables, pltpu.SMEM), (far, pltpu.HBM), (near, pltpu.VMEM)):
        operands += [pltpu.with_memory_space_constraint(v, place) for v in values]
        places += [SPEC[place]] * len(values)
    shapes = []
    for shape, dtype, place in outs:
        shapes.append(place(shape, dtype) if place else jax.ShapeDtypeStruct(shape, dtype))
    return pl.pallas_call(
        kernel,
        out_shape=shapes,
        in_specs=places,
        out_specs=[SPEC[place or pltpu.VMEM] for _, _, place in outs],
        scratch_shapes=list(scratch),
        compiler_params=pltpu.CompilerParams(vmem_limit_bytes=LIMIT),
    )(*operands)


def shards(leaf_parents, mid_parents, leaf_codes, mid_codes, leaf_valid, mid_valid,
           leaf_inverse, mid_inverse, top_inverse, leaf_panels, mid_panels,
           leaf_cotangent, mid_cotangent, top_cotangent, mid_primal, top_primal):
    nl, probes, width = leaf_cotangent.shape
    nm = mid_cotangent.shape[0]
    nt = top_cotangent.shape[0]
    rows = leaf_panels.shape[1]
    leaves = lax.axis_size("leaf")
    peers = lax.axis_size("rhs")
    groups = peers // 2
    assert leaf_codes.shape[1] == 1 and mid_codes.shape[1] == 1 and rows == BLK
    tables = (leaf_parents, mid_parents, leaf_codes.reshape(-1), mid_codes.reshape(-1),
              leaf_valid, mid_valid)
    load = FAN + nl + nm

    def along(value, first, stride):
        return lax.ppermute(value, "leaf", swaps(leaves, first, stride))

    def core_swap(value):
        return lax.ppermute(value, "rhs", [(i, i ^ 1) for i in range(peers)])

    def near(shape, dtype):
        return (shape, dtype, pltpu.VMEM)

    def same(value):
        return near(value.shape, value.dtype)

    piece = (probes, BLK)
    tprim_x = core_swap(top_primal)
    moved = (mid_primal, top_primal, mid_cotangent, mid_inverse, mid_panels, top_cotangent,
             top_inverse)
    (*tables, leaf_adj, upd, send_z, send_y, mprim, tprim, mid_cot, mid_inv, mid_pan,
     top_cot, top_inv) = call(
        leaf_kernel, (),
        (*tables, leaf_cotangent, leaf_inverse, leaf_panels, *moved), (),
        [*((t.shape, t.dtype, pltpu.SMEM) for t in tables),
         near((nl, probes, width), BF16), near((nl, *piece), F32), near((load, *piece), BF16),
         near((load, *piece), BF16), *map(same, moved)],
        [pltpu.VMEM(v.shape, v.dtype) for v in (leaf_cotangent, leaf_inverse, leaf_panels)]
        + [DMA((1 + 2 * nl + len(moved),)), DMA((len(tables),))],
    )
    rec_z = along(send_z, 1, 1)
    rec_y = along(send_y, 0, 1)
    far_a, far_b = call(
        lambda *refs: far_kernel(nl, nm, *refs), tables, (), (tprim, tprim_x),
        [near((FAN, 2 * probes, BLK), BF16)] * 2,
    )
    far_a = along(far_a, 0, 2)
    far_b = along(far_b, 1, 2)
    leaf_other = core_swap(leaf_adj)
    mid_adj, pack, send_z, send_y, keep = call(
        mid_kernel, tables, (),
        (rec_z, rec_y, upd, mid_cot, mid_inv, mid_pan, mprim, tprim),
        [near((nm, probes, width), BF16), near((nl + nm + nm * NB, *piece), BF16),
         near((nt * NB, *piece), BF16), near((nt * NB, *piece), BF16),
         near((nt * NB, *piece), F32)],
        [pltpu.VMEM((nm * NB + 3 * nt * NB + 1, *piece), F32)],
    )
    rec_z = along(send_z, 1, 1)
    rec_y = along(send_y, 0, 1)
    pack_other = core_swap(pack)
    part = (rows // peers, width)
    leaf_sum, mid_sum, *sends = call(
        lambda *refs: grad_kernel(groups, *refs), tables, (),
        (far_a, far_b, leaf_adj, leaf_other, pack, pack_other),
        [near((nl, *part), F32), near((nm, *part), F32)]
        + [near((nl + nm, *part), BF16)] * (groups - 1),
        [pltpu.VMEM((nl + nm, rows, 2 * probes), F32)],
    )
    leaf_out, mid_out = call(
        out_kernel, (), (), (leaf_adj, mid_adj),
        [((nl, probes, width), BF16, pltpu.HBM), ((nm, probes, width), BF16, pltpu.HBM)],
        [DMA((2,))],
    )
    gets = []
    for step, value in enumerate(sends, 1):
        pairs = [(i, (i // 2 + step) % groups * 2 + i % 2) for i in range(peers)]
        gets.append(lax.ppermute(value, "rhs", pairs))
    top_adj, leaf_grad, mid_grad = call(
        last_kernel, (), (),
        (keep, rec_z, rec_y, top_cot, top_inv, leaf_sum, mid_sum, *gets),
        [((nt, probes, width), BF16, None), ((nl, *part), BF16, None), ((nm, *part), BF16, None)],
    )
    return leaf_out, mid_out, top_adj, leaf_grad, mid_grad


def solution(mesh):
    each = P("leaf")
    block = P("leaf", None, None)
    split = P("leaf", "rhs", None)

    return jax.shard_map(
        shards,
        mesh=mesh,
        in_specs=(P(),) * 4 + (each,) * 2 + (block,) * 5 + (split,) * 5,
        out_specs=(split,) * 5,
        check_vma=False,
    )
```

```python
import jax
import jax.numpy as jnp
from jax import lax
from jax.experimental import pallas as pl
from jax.experimental.pallas import tpu as pltpu
from jax.sharding import PartitionSpec as P


BLK = 128
NB = 4
FAN = 2
LIMIT = 16 << 20
BF16 = jnp.bfloat16
F32 = jnp.float32


def dot_t(a, b):
    return lax.dot_general(a, b, (((1,), (1,)), ((), ())), preferred_element_type=F32)


def div(a, b):
    return lax.div(a, jnp.int32(b))


def swaps(size, first, stride):
    pairs = []
    for i in range(size):
        block = i // stride
        other = i + stride if (block - first) % 2 == 0 else i - stride
        if 0 <= other < size:
            pairs.append((i, other))
    return pairs


def partner(d, first, stride):
    block = div(d, stride)
    return jnp.where((block - first) % 2 == 0, d + stride, d - stride)


def clip(i, size):
    return jnp.minimum(jnp.maximum(i, 0), size - 1)


class Tables:
    def __init__(self, lp, mp, lc, mc, nl, nm, nt):
        self.lp, self.mp, self.lc, self.mc = lp, mp, lc, mc
        self.nl, self.nm, self.nt = nl, nm, nt

    def leaf(self, s):
        s = clip(s, self.lp.shape[0])
        p = self.lp[s]
        code = self.lc[s]
        q = self.mp[p]
        return p, q, code

    def leaf_source(self, s):
        p, q, code = self.leaf(s)
        near = code < NB
        device = jnp.where(near, div(p, self.nm), div(q, self.nt))
        row = jnp.where(near, p - div(p, self.nm) * self.nm, q - div(q, self.nt) * self.nt)
        return near, device, row, jnp.where(near, code, code - NB)

    def mid_source(self, m):
        m = clip(m, self.mp.shape[0])
        q = self.mp[m]
        return div(q, self.nt), q - div(q, self.nt) * self.nt, self.mc[m]


def block_of(ref, row, blk):
    return ref[row, :, pl.ds(pl.multiple_of(blk * BLK, BLK), BLK)]


def leaf_pick(tabs, s, mprim, tprim):
    near, _, row, blk = tabs.leaf_source(s)
    a = block_of(mprim, jnp.where(near, row, 0), blk)
    b = block_of(tprim, jnp.where(near, 0, row), blk)
    return jnp.where(near, a, b)


def mid_pick(tabs, m, tprim):
    _, row, blk = tabs.mid_source(m)
    return block_of(tprim, row, blk)


def move(sems, pairs):
    copies = [pltpu.make_async_copy(*pair, sems.at[i]) for i, pair in enumerate(pairs)]
    for copy in copies:
        copy.start()
    return copies


def leaf_kernel(lp_h, mp_h, lc_h, mc_h, lv_h, mv_h, cot_h, inv_h, pan_h, mprim_h, tprim_h,
                later_a, later_b, later_c, later_d, later_e, lp, mp, lc, mc, lv, mv,
                adj, upd, send_z, send_y, mprim, tprim,
                out_a, out_b, out_c, out_d, out_e, cot, inv, pan, sems, table_sems):
    nl, nm, nt = cot.shape[0], mprim.shape[0], tprim.shape[0]
    tables = [(lp_h, lp), (mp_h, mp), (lc_h, lc), (mc_h, mc), (lv_h, lv), (mv_h, mv)]
    reads = move(table_sems, tables)
    pairs = [(mprim_h, mprim), (tprim_h, tprim), (cot_h, cot)]
    pairs += [(inv_h.at[s], inv.at[s]) for s in range(nl)]
    pairs += [(pan_h.at[s], pan.at[s]) for s in range(nl)]
    pairs += [(later_a, out_a), (later_b, out_b), (later_c, out_c), (later_d, out_d),
              (later_e, out_e)]
    copies = move(sems, pairs)
    d = lax.axis_index("leaf")
    tabs = Tables(lp, mp, lc, mc, nl, nm, nt)
    col = lax.broadcasted_iota(jnp.int32, upd.shape[1:], 1)

    def picks(out, first):
        t = partner(d, first, 1)
        for i in range(nl):
            out[FAN + i] = leaf_pick(tabs, t * nl + i, mprim, tprim)
        for i in range(nm):
            out[FAN + nl + i] = mid_pick(tabs, t * nm + i, tprim)

    for copy in reads + copies[:2]:
        copy.wait()
    picks(send_z, 1)
    picks(send_y, 0)
    for copy in copies[2:3 + nl // 2]:
        copy.wait()
    for s in range(nl // 2):
        adj[s] = dot_t(cot[s], inv[s]).astype(BF16)
    for copy in copies[3 + nl // 2:3 + 2 * nl]:
        copy.wait()
    for s in range(nl // 2, nl):
        adj[s] = dot_t(cot[s], inv[s]).astype(BF16)
    for s in range(nl):
        upd[s] = jnp.where(col < lv[s], dot_t(adj[s], pan[s]), 0.0)
    for out, first in ((send_z, 1), (send_y, 0)):
        start = jnp.where(partner(d, first, 1) > d, nl - FAN, 0)
        for i in range(FAN):
            out[i] = upd[start + i].astype(BF16)
    for copy in copies[3 + 2 * nl:]:
        copy.wait()


def far_kernel(nl, nm, lp, mp, lc, mc, lv, mv, tprim, tprim_x, far_a, far_b):
    nt = tprim.shape[0]
    probes = tprim.shape[1]
    d = lax.axis_index("leaf")
    tabs = Tables(lp, mp, lc, mc, nl, nm, nt)
    for out, first in ((far_a, 0), (far_b, 1)):
        t = partner(d, first, 2)
        start = jnp.where(t > d, 0, nl - FAN)
        for i in range(FAN):
            _, _, row, blk = tabs.leaf_source(t * nl + start + i)
            row = jnp.minimum(row, nt - 1)
            out[i, :probes] = block_of(tprim, row, blk)
            out[i, probes:] = block_of(tprim_x, row, blk)


def mid_kernel(lp, mp, lc, mc, lv, mv, rec_z, rec_y, upd, cot, inv, pan,
               mprim, tprim, adj, pack, send_z, send_y, keep, acc):
    nl, nm, nt = upd.shape[0], mprim.shape[0], tprim.shape[0]
    d = lax.axis_index("leaf")
    tabs = Tables(lp, mp, lc, mc, nl, nm, nt)
    base = nm * NB
    dump = base + 3 * nt * NB
    for m in range(nm):
        for k in range(NB):
            acc[m * NB + k] = cot[m, :, k * BLK:(k + 1) * BLK].astype(F32)
    for k in range(base, dump):
        acc[k] = jnp.zeros(acc.shape[1:], F32)
    total = lp.shape[0]

    def top_slot(q, k):
        return clip(base + (q - (d - 1) * nt) * NB + k, dump)

    def take(s, value):
        p, q, code = tabs.leaf(s)
        mine = (s >= 0) & (s < total) & (div(p, nm) == d)
        slot = jnp.where(code < NB, (p - d * nm) * NB + code, top_slot(q, code - NB))
        slot = jnp.where(mine, clip(slot, dump), dump)
        acc[slot] = acc[slot] - value

    for i in range(nl):
        take(d * nl + i, upd[i])
    near = []
    for rec, first in ((rec_z, 1), (rec_y, 0)):
        t = partner(d, first, 1)
        near.append((t, rec))
        start = jnp.where(t > d, t * nl, (t + 1) * nl - FAN)
        for i in range(FAN):
            take(start + i, rec[i].astype(F32))
    col = lax.broadcasted_iota(jnp.int32, acc.shape[1:], 1)
    solved, updates = [], []
    for m in range(nm):
        rhs = jnp.concatenate([acc[m * NB + k].astype(BF16) for k in range(NB)], axis=1)
        solved.append(dot_t(rhs, inv[m]).astype(BF16))
    for m in range(nm):
        updates.append(jnp.where(col < mv[m], dot_t(solved[m], pan[m]), 0.0))
    for m in range(nm):
        p = d * nm + m
        slot = top_slot(mp[p], mc[p])
        acc[slot] = acc[slot] - updates[m]
    for out, (t, _) in ((send_z, near[0]), (send_y, near[1])):
        for k in range(nt * NB):
            out[k] = acc[base + (t - d + 1) * nt * NB + k].astype(BF16)
    for k in range(nt * NB):
        keep[k] = acc[base + nt * NB + k]
    for m in range(nm):
        adj[m] = solved[m]
        for k in range(NB):
            pack[nl + nm + m * NB + k] = solved[m][:, k * BLK:(k + 1) * BLK]
    for i in range(nl):
        _, dev, _, _ = tabs.leaf_source(d * nl + i)
        value = leaf_pick(tabs, d * nl + i, mprim, tprim)
        for t, rec in near:
            value = jnp.where(dev == t, rec[FAN + i], value)
        pack[i] = jnp.where(col < lv[i], value, jnp.zeros_like(value))
    for i in range(nm):
        dev, _, _ = tabs.mid_source(d * nm + i)
        value = mid_pick(tabs, d * nm + i, tprim)
        for t, rec in near:
            value = jnp.where(dev == t, rec[FAN + nl + i], value)
        pack[nl + i] = jnp.where(col < mv[i], value, jnp.zeros_like(value))


def grad_kernel(groups, lp, mp, lc, mc, lv, mv, far_a, far_b, leaf_own, leaf_other,
                rows_own, rows_other, keep_leaf, keep_mid, *rest):
    sends, cols = rest[:-1], rest[-1]
    nl, nm = leaf_own.shape[0], keep_mid.shape[0]
    d, j = lax.axis_index("leaf"), lax.axis_index("rhs")
    tabs = Tables(lp, mp, lc, mc, nl, nm, nm // FAN)
    both_probes = FAN * rows_own.shape[1]
    col = lax.broadcasted_iota(jnp.int32, (both_probes, BLK), 1)
    unit = (lax.broadcasted_iota(jnp.int32, (both_probes, both_probes), 0)
            == lax.broadcasted_iota(jnp.int32, (both_probes, both_probes), 1))
    unit = unit.astype(F32).astype(BF16)
    x = div(j, 2)
    far = ((partner(d, 0, 2), far_a), (partner(d, 1, 2), far_b))
    width = keep_leaf.shape[1]
    for s in range(nl + nm):
        both = jnp.concatenate([rows_own[s], rows_other[s]], axis=0)
        if s < nl:
            _, dev, _, _ = tabs.leaf_source(d * nl + s)
            for t, rec in far:
                take = (dev == t) & (col < lv[s])
                if s < FAN:
                    both = jnp.where(take & (t < d), rec[s], both)
                if s >= nl - FAN:
                    both = jnp.where(take & (t > d), rec[s - nl + FAN], both)
        cols[s] = lax.dot_general(
            both, unit, (((0,), (0,)), ((), ())), preferred_element_type=F32
        )
    for s in range(nl + nm):
        keep, i = (keep_leaf, s) if s < nl else (keep_mid, s - nl)
        if s < nl:
            adj = jnp.concatenate([leaf_own[s], leaf_other[s]], axis=0)
        else:
            blocks = [nl + nm + i * NB + k for k in range(NB)]
            adj = jnp.concatenate([jnp.concatenate([ref[b] for b in blocks], axis=1)
                                   for ref in (rows_own, rows_other)], axis=0)
        picked = [cols[s, pl.ds(pl.multiple_of(j * width, width), width), :]]
        for step in range(1, groups):
            to = (x + step) % groups * 2 + j % 2
            picked.append(cols[s, pl.ds(pl.multiple_of(to * width, width), width), :])
        value = lax.dot_general(
            jnp.concatenate(picked, axis=0).astype(BF16), adj, (((1,), (0,)), ((), ())),
            preferred_element_type=F32,
        )
        keep[i] = value[:width]
        for step, out in enumerate(sends, 1):
            out[s] = value[step * width:(step + 1) * width].astype(BF16)


def out_kernel(*refs):
    refs, sems = refs[:-1], refs[-1]
    half = len(refs) // 2
    for copy in move(sems, list(zip(refs[:half], refs[half:]))):
        copy.wait()


def last_kernel(keep, rec_z, rec_y, cot, inv, leaf_sum, mid_sum, *rest):
    gets, (adj, leaf_out, mid_out) = rest[:-3], rest[-3:]
    nl = leaf_sum.shape[0]
    for total, out, first in ((leaf_sum, leaf_out, 0), (mid_sum, mid_out, nl)):
        for i in range(total.shape[0]):
            value = total[i]
            for get in gets:
                value = value + get[first + i].astype(F32)
            out[i] = (-value).astype(BF16)
    for q in range(cot.shape[0]):
        parts = []
        for k in range(NB):
            total = keep[q * NB + k] + rec_z[q * NB + k].astype(F32) + rec_y[q * NB + k].astype(F32)
            total = total + cot[q, :, k * BLK:(k + 1) * BLK].astype(F32)
            parts.append(total.astype(BF16))
        adj[q] = dot_t(jnp.concatenate(parts, axis=1), inv[q]).astype(BF16)


SPEC = {m: pl.BlockSpec(memory_space=m) for m in (pltpu.SMEM, pltpu.VMEM, pltpu.HBM)}
DMA = pltpu.SemaphoreType.DMA


def call(kernel, tables, far, near, outs, scratch=()):
    operands, places = [], []
    for values, place in ((tables, pltpu.SMEM), (far, pltpu.HBM), (near, pltpu.VMEM)):
        operands += [pltpu.with_memory_space_constraint(v, place) for v in values]
        places += [SPEC[place]] * len(values)
    shapes = []
    for shape, dtype, place in outs:
        shapes.append(place(shape, dtype) if place else jax.ShapeDtypeStruct(shape, dtype))
    return pl.pallas_call(
        kernel,
        out_shape=shapes,
        in_specs=places,
        out_specs=[SPEC[place or pltpu.VMEM] for _, _, place in outs],
        scratch_shapes=list(scratch),
        compiler_params=pltpu.CompilerParams(vmem_limit_bytes=LIMIT),
    )(*operands)


def shards(leaf_parents, mid_parents, leaf_codes, mid_codes, leaf_valid, mid_valid,
           leaf_inverse, mid_inverse, top_inverse, leaf_panels, mid_panels,
           leaf_cotangent, mid_cotangent, top_cotangent, mid_primal, top_primal):
    nl, probes, width = leaf_cotangent.shape
    nm = mid_cotangent.shape[0]
    nt = top_cotangent.shape[0]
    rows = leaf_panels.shape[1]
    leaves = lax.axis_size("leaf")
    peers = lax.axis_size("rhs")
    groups = peers // 2
    assert leaf_codes.shape[1] == 1 and mid_codes.shape[1] == 1 and rows == BLK
    tables = (leaf_parents, mid_parents, leaf_codes.reshape(-1), mid_codes.reshape(-1),
              leaf_valid, mid_valid)
    load = FAN + nl + nm

    def along(value, first, stride):
        return lax.ppermute(value, "leaf", swaps(leaves, first, stride))

    def core_swap(value):
        return lax.ppermute(value, "rhs", [(i, i ^ 1) for i in range(peers)])

    def near(shape, dtype):
        return (shape, dtype, pltpu.VMEM)

    def same(value):
        return near(value.shape, value.dtype)

    piece = (probes, BLK)
    tprim_x = core_swap(top_primal)
    moved = (mid_primal, top_primal, mid_cotangent, mid_inverse, mid_panels, top_cotangent,
             top_inverse)
    (*tables, leaf_adj, upd, send_z, send_y, mprim, tprim, mid_cot, mid_inv, mid_pan,
     top_cot, top_inv) = call(
        leaf_kernel, (),
        (*tables, leaf_cotangent, leaf_inverse, leaf_panels, *moved), (),
        [*((t.shape, t.dtype, pltpu.SMEM) for t in tables),
         near((nl, probes, width), BF16), near((nl, *piece), F32), near((load, *piece), BF16),
         near((load, *piece), BF16), *map(same, moved)],
        [pltpu.VMEM(v.shape, v.dtype) for v in (leaf_cotangent, leaf_inverse, leaf_panels)]
        + [DMA((1 + 2 * nl + len(moved),)), DMA((len(tables),))],
    )
    rec_z = along(send_z, 1, 1)
    rec_y = along(send_y, 0, 1)
    far_a, far_b = call(
        lambda *refs: far_kernel(nl, nm, *refs), tables, (), (tprim, tprim_x),
        [near((FAN, 2 * probes, BLK), BF16)] * 2,
    )
    far_a = along(far_a, 0, 2)
    far_b = along(far_b, 1, 2)
    leaf_other = core_swap(leaf_adj)
    mid_adj, pack, send_z, send_y, keep = call(
        mid_kernel, tables, (),
        (rec_z, rec_y, upd, mid_cot, mid_inv, mid_pan, mprim, tprim),
        [near((nm, probes, width), BF16), near((nl + nm + nm * NB, *piece), BF16),
         near((nt * NB, *piece), BF16), near((nt * NB, *piece), BF16),
         near((nt * NB, *piece), F32)],
        [pltpu.VMEM((nm * NB + 3 * nt * NB + 1, *piece), F32)],
    )
    rec_z = along(send_z, 1, 1)
    rec_y = along(send_y, 0, 1)
    pack_other = core_swap(pack)
    part = (rows // peers, width)
    leaf_sum, mid_sum, *sends = call(
        lambda *refs: grad_kernel(groups, *refs), tables, (),
        (far_a, far_b, leaf_adj, leaf_other, pack, pack_other),
        [near((nl, *part), F32), near((nm, *part), F32)]
        + [near((nl + nm, *part), BF16)] * (groups - 1),
        [pltpu.VMEM((nl + nm, rows, 2 * probes), F32)],
    )
    leaf_out, mid_out = call(
        out_kernel, (), (), (leaf_adj, mid_adj),
        [((nl, probes, width), BF16, pltpu.HBM), ((nm, probes, width), BF16, pltpu.HBM)],
        [DMA((2,))],
    )
    gets = []
    for step, value in enumerate(sends, 1):
        pairs = [(i, (i // 2 + step) % groups * 2 + i % 2) for i in range(peers)]
        gets.append(lax.ppermute(value, "rhs", pairs))
    top_adj, leaf_grad, mid_grad = call(
        last_kernel, (), (),
        (keep, rec_z, rec_y, top_cot, top_inv, leaf_sum, mid_sum, *gets),
        [((nt, probes, width), BF16, None), ((nl, *part), BF16, None), ((nm, *part), BF16, None)],
    )
    return leaf_out, mid_out, top_adj, leaf_grad, mid_grad


def solution(mesh):
    each = P("leaf")
    block = P("leaf", None, None)
    split = P("leaf", "rhs", None)

    return jax.shard_map(
        shards,
        mesh=mesh,
        in_specs=(P(),) * 4 + (each,) * 2 + (block,) * 5 + (split,) * 5,
        out_specs=(split,) * 5,
        check_vma=False,
    )
```
